32 devices in a mesh: energy: 4 (over y, x), space: 8 (over z, core).
Axes of the slice: x: 2, y: 2, z: 4, core: 2. Of those that a mesh axis runs over, the one named last changes fastest.
Arguments:
- right_side: float32 [4, 64, 64, 512], P(None, 'space', None, 'energy')
- rate: float32 [64, 64, 512], P('space', None, 'energy'), may hold values from 0.5 to 2
- fields: float32 [2, 64, 64], P(None, 'space'), may hold values from -3 to 3
- speed: float32 [512], P('energy'), may hold values from 0.3 to 1
- regions: int32 [64, 64], P('space'), may hold values from 0 to 3
- contacts: int32 [64, 64], P('space'), may hold values 0 or 1
- offsets: int32 [4], replicated, may hold values from 12 to 24, as said below
- phonon: float32 [4, 2], replicated, may hold values from 0.1 to 0.6
Outputs:
- state: float32 [4, 64, 64, 512], P(None, 'space', None, 'energy')
- norms: float32 [2, 4], replicated
The draws below stay inside these ranges and needn't reach their ends.
Inputs may be any that keep to these rules, and one draw needn't show every extreme that they name: `offsets`: each region's phonon energy lies between 12 and 24 bins; some region has exactly 24.
All inputs are finite; a program needn't handle non-finite values. No bound on the sum of `contacts` on one device may be relied on, other than what follows from the above.
Results may differ from the reference program's by a relative error of at most 0.0001.
Values sent between devices are 32-bit elements; how exact they have to be, the bound alone decides.
A program may use at most 64 MiB of HBM per device.

```python
import math
import jax
import jax.numpy as jnp
from jax import lax

COEFS = 4
Y = 64
HOP = 24
REGIONS = 4
SWEEPS = 2
X = 64
E = 512


def draw_right_side(key, part):
    xs = jnp.arange(X, dtype=jnp.float32) / max(X - 1, 1)
    es = jnp.arange(E, dtype=jnp.float32) / max(E - 1, 1)
    profile = (1.0 + 2.0 * xs)[:, None, None] * (1.0 + 2.0 * es)[None, None, :]
    base = jax.random.normal(jax.random.fold_in(key, 1), (COEFS, X, Y, E), dtype=jnp.float32)
    return (base * profile[None]).astype(jnp.float32)


def draw_offsets(key, part):
    values = jax.random.randint(jax.random.fold_in(key, 5), (REGIONS,), HOP // 2, HOP + 1)
    where_top = jax.random.randint(jax.random.fold_in(key, 6), (), 0, REGIONS)
    return jnp.where(jnp.arange(REGIONS) == where_top, HOP, values).astype(jnp.int32)


def touch_ends(entries, rng, smallest, top_value):
    dims = entries.shape
    place = [jax.random.randint(jax.random.fold_in(rng, axis), (), 0, dims[axis]) for axis in range(len(dims))]
    entries = entries.at[tuple(place)].set(smallest)
    longest = dims.index(max(dims))
    place[longest] = (place[longest] + 1) % dims[longest]
    return entries.at[tuple(place)].set(top_value)


def shard_levels(rng, extent, cuts, smallest, high):
    level = 1.0
    for axis_at, parts in cuts:
        heights = jax.random.uniform(jax.random.fold_in(jax.random.fold_in(rng, 6), axis_at), (parts,), jnp.float32, smallest / len(cuts), high / len(cuts))
        level = level * jnp.repeat(jnp.exp(heights), extent[axis_at] // parts).reshape((-1,) + (1,) * (len(extent) - 1 - axis_at))
    return level


def centred(key, dims, scale, limit, pieces=(), held_as=jnp.bfloat16):
    result = scale * jax.random.normal(key, dims, jnp.float32)
    if pieces:
        result = result * shard_levels(key, dims, pieces, -0.22, 0.18)
    return jnp.clip(result, -limit, limit).astype(held_as)


def setup_inputs(seed: int = 0) -> dict:
    key_of = jax.random.split(jax.random.key(seed), 9)
    right_side = draw_right_side(jax.random.fold_in(key_of[8], 71), 0)
    rate = jnp.clip(jnp.exp(math.log(2.0) - 1.3862944 * jax.random.uniform(key_of[1], (X, Y, E), jnp.float32) ** shard_levels(key_of[1], (X, Y, E), ((0, 8), (2, 4)), -0.2, 0.2)), 0.5, 2.0)
    fields = centred(key_of[2], (2, X, Y), 0.5, 3.0, ((1, 8),), jnp.float32)
    speed = jnp.clip(jnp.exp(math.log(1.0) - 1.2039728 * jax.random.uniform(key_of[3], (E,), jnp.float32) ** shard_levels(key_of[3], (E,), ((0, 4),), -0.2, 0.2)), 0.3, 1.0)
    regions = touch_ends(jax.random.randint(key_of[4], (X, Y), 0, REGIONS), jax.random.fold_in(key_of[4], 1), 0, REGIONS - 1).astype(jnp.int32)
    contacts = touch_ends((jax.random.randint(key_of[5], (X, Y), 0, 8) < 1).astype(jnp.int32), jax.random.fold_in(key_of[5], 1), 0, 1)
    offsets = draw_offsets(jax.random.fold_in(key_of[8], 71), 0)
    phonon = jnp.clip(jnp.exp(jax.random.uniform(key_of[7], (REGIONS, 2), jnp.float32, math.log(0.1), math.log(0.6))), 0.1, 0.6)
    return {"right_side": right_side, "rate": rate, "fields": fields, "speed": speed, "regions": regions, "contacts": contacts, "offsets": offsets, "phonon": phonon}


diffusion = 0.25

def operator_of(field, diagonal, push_x, push_y, speed, regions, offsets, phonon):
    padded_x = jnp.pad(field, ((0, 0), (1, 1), (0, 0), (0, 0)))
    after_x = padded_x[:, 2:]
    before_x = padded_x[:, :-2]
    padded_y = jnp.pad(field, ((0, 0), (0, 0), (1, 1), (0, 0)))
    after_y = padded_y[:, :, 2:]
    before_y = padded_y[:, :, :-2]
    beside = after_x + before_x + after_y + before_y
    velocity = speed[None, None, :]
    drift_zero = 0.5 * velocity * (after_x[1] - before_x[1] + (after_y[2] - before_y[2]))
    drift_one = 0.5 * velocity * (after_x[0] - before_x[0])
    drift_two = 0.5 * velocity * (after_y[0] - before_y[0])
    width = field.shape[3]
    padded_e = jnp.pad(field[0], ((0, 0), (0, 0), (HOP, HOP)))
    scatter = jnp.zeros_like(field[0])
    for region in range(REGIONS):
        below = lax.dynamic_slice_in_dim(padded_e, (HOP - offsets[region]).astype(jnp.int32), width, 2)
        above = lax.dynamic_slice_in_dim(padded_e, (HOP + offsets[region]).astype(jnp.int32), width, 2)
        inside = (regions == region).astype(field.dtype)[:, :, None]
        scatter = scatter + inside * (phonon[region, 0] * below + phonon[region, 1] * above)
    out_zero = diagonal * field[0] + push_x * field[1] + push_y * field[2] - diffusion * beside[0] + drift_zero - scatter
    out_one = -push_x * field[0] + diagonal * field[1] - diffusion * beside[1] + drift_one
    out_two = -push_y * field[0] + diagonal * field[2] - diffusion * beside[2] + drift_two
    out_three = diagonal * field[3] - diffusion * beside[3]
    return jnp.stack([out_zero, out_one, out_two, out_three])

def block_solve(resid, diagonal, push_x, push_y):
    first = (diagonal * resid[0] - push_x * resid[1] - push_y * resid[2]) / (diagonal * diagonal + push_x * push_x + push_y * push_y)
    second = (resid[1] + push_x * first) / diagonal
    third = (resid[2] + push_y * first) / diagonal
    fourth = resid[3] / diagonal
    return jnp.stack([first, second, third, fourth])

def reference(right_side, rate, fields, speed, regions, contacts, offsets, phonon):
    diagonal = rate + 4.0 * diffusion
    push_x = fields[0][:, :, None]
    push_y = fields[1][:, :, None]
    pinned = (contacts == 1)[None, :, :, None]
    state = jnp.zeros_like(right_side)
    resid = right_side
    norm_rows = []
    for sweep in range(SWEEPS):
        solved = block_solve(resid, diagonal, push_x, push_y)
        state = state + jnp.where(pinned, resid, solved)
        image = operator_of(state, diagonal, push_x, push_y, speed, regions, offsets, phonon)
        resid = jnp.where(pinned, right_side - state, right_side - image)
        norm_rows.append(jnp.sqrt(lax.optimization_barrier(jnp.sum(resid * resid, axis=(1, 2, 3)))))
    return (state, jnp.stack(norm_rows))
```

```python
import functools

import jax
import jax.numpy as jnp
from jax import lax
from jax.experimental import pallas as pl
from jax.experimental.pallas import tpu as pltpu
from jax.sharding import PartitionSpec as P

HOP = 24
REGIONS = 4
SWEEPS = 2
COEFS = 4
PAD = 8
ROWS = 16
UNIT = 8

diffusion = 0.25

MESH = pl.DeviceIdType.MESH


def kernel(
    n_energy,
    n_space,
    offsets_hbm,
    phonon_hbm,
    right_hbm,
    rate_hbm,
    fields_hbm,
    speed_hbm,
    regions_hbm,
    contacts_hbm,
    state_ref,
    sums_ref,
    offsets_ref,
    phonon_ref,
    fields_ref,
    speed_ref,
    regions_ref,
    contacts_ref,
    right,
    rate,
    field_0,
    field_1,
    part,
    halo,
    cell_x,
    cell_y,
    cell_pin,
    cell_off,
    cell_absorb,
    cell_emit,
    inv_diag,
    inv_det,
    turn_low,
    turn_high,
    gain_low,
    gain_high,
    pack_low,
    pack_high,
    from_low,
    from_high,
    sums,
    in_sem,
    out_sem,
    x_send,
    x_recv,
    e_send,
    e_recv,
    n_send,
    n_recv,
    known,
):
    nx, ny, width = right.shape[1:]
    groups = width // HOP
    tall = ny // UNIT
    field = (field_0, field_1)
    chunks = chunks_of(nx)
    spans = spans_of(chunks, tall, groups)
    e = lax.axis_index("energy")
    s = lax.axis_index("space")
    me = e * n_space + s

    barrier = pltpu.get_barrier_semaphore()
    for step in range(1, n_energy):
        pl.semaphore_signal(
            barrier,
            inc=1,
            device_id=(lax.rem(e + step, n_energy), s),
            device_id_type=MESH,
        )
    for step in range(1, n_space):
        pl.semaphore_signal(
            barrier,
            inc=1,
            device_id=(e, lax.rem(s + step, n_space)),
            device_id_type=MESH,
        )

    def plane_at(i):
        turned, step = lax.rem(i, 2), lax.div(i, 2)
        return step + turned * (nx - 1 - 2 * step)

    def plane_of(i):
        return i // 2 if i % 2 == 0 else nx - 1 - i // 2

    small = [
        pltpu.make_async_copy(source, target, in_sem.at[i])
        for i, (source, target) in enumerate(
            (
                (fields_hbm, fields_ref),
                (contacts_hbm, contacts_ref),
                (offsets_hbm, offsets_ref),
                (phonon_hbm, phonon_ref),
                (regions_hbm, regions_ref),
                (speed_hbm, speed_ref),
            )
        )
    ]
    load_rate = pltpu.make_async_copy(rate_hbm, rate, in_sem.at[6])
    load_right = [
        pltpu.make_async_copy(
            right_hbm.at[:, plane_of(i)], right.at[:, plane_of(i)], in_sem.at[7 + i]
        )
        for i in range(nx)
    ]
    for load in (*small, load_rate, *load_right):
        load.start()

    zero_rows = jnp.zeros((PAD, width), jnp.float32)
    zero_plane = jnp.zeros((ny, width), jnp.float32)
    for k in range(SWEEPS):
        for c in range(COEFS):
            for x in range(1, nx + 1):
                field[k][c, x, 0:PAD] = zero_rows
                field[k][c, x, PAD + ny : 2 * PAD + ny] = zero_rows
            field[k][c, 0, PAD : PAD + ny] = zero_plane
            field[k][c, nx + 1, PAD : PAD + ny] = zero_plane

    @pl.when(e == 0)
    def _():
        for k in range(SWEEPS):
            from_low[k] = jnp.zeros(from_low.shape[1:], jnp.float32)

    @pl.when(e == n_energy - 1)
    def _():
        for k in range(SWEEPS):
            from_high[k] = jnp.zeros(from_high.shape[1:], jnp.float32)

    for load in small:
        load.wait()

    region = regions_ref[...]
    free = contacts_ref[...] != 1
    off = jnp.zeros_like(region)
    absorb = jnp.zeros(region.shape, jnp.float32)
    emit = jnp.zeros(region.shape, jnp.float32)
    for r in range(REGIONS):
        inside = region == r
        off = jnp.where(inside, offsets_ref[r], off)
        absorb = jnp.where(inside & free, phonon_ref[0, r], absorb)
        emit = jnp.where(inside & free, phonon_ref[1, r], emit)

    def spread(*pairs):
        for source, target in pairs:
            turned = source.T
            for x in range(nx):
                target[x] = jnp.broadcast_to(turned[:, x : x + 1], (ny, width))

    spread(
        (fields_ref[0], cell_x),
        (fields_ref[1], cell_y),
        (contacts_ref[...], cell_pin),
        (off, cell_off),
        (absorb, cell_absorb),
        (emit, cell_emit),
    )

    def solve(r, px, py, diag, inv_d, inv_t):
        first = (diag * r[0] - px * r[1] - py * r[2]) * inv_t
        return (
            first,
            (r[1] + px * first) * inv_d,
            (r[2] + py * first) * inv_d,
            r[3] * inv_d,
        )

    lane = lax.broadcasted_iota(jnp.int32, (ROWS, width), 1)
    unit_lane = lax.broadcasted_iota(jnp.int32, (UNIT, width), 1)

    def slot(at):
        at = at % width
        return (unit_lane >= at) & (unit_lane < at + HOP)

    slot_low = [slot(HOP * j) for j in range(groups)]
    slot_high = [slot(HOP * (j - 1)) for j in range(groups)]
    zero = jnp.zeros((UNIT, width), jnp.float32)

    def turn(value, by):
        by = by % width
        return pltpu.roll(value, by, 1) if by else value

    def units_of(g):
        first, last = chunks[g]
        units = [(plane_of(i), y) for i in range(first, last) for y in range(0, ny, UNIT)]
        start = spans[g][0]
        return [(start + u // groups, u % groups, *unit) for u, unit in enumerate(units)]

    def rotated(f, off):
        low, high = lane < off, lane >= width - off
        below = jnp.take_along_axis(
            f,
            jnp.where(low, lane - off + width, lane - off),
            axis=1,
            mode="promise_in_bounds",
        )
        above = jnp.take_along_axis(
            f,
            jnp.where(high, lane + off - width, lane + off),
            axis=1,
            mode="promise_in_bounds",
        )
        return jnp.where(low, 0.0, below), jnp.where(high, 0.0, above)

    def pack(k, g):
        low, high = zero, zero
        units = units_of(g)
        for u, (q, j, x, y) in enumerate(units):
            turned = turn(field[k][0, x + 1, pl.ds(PAD + y, UNIT)], HOP * j)
            low = jnp.where(slot_low[j], turned, low)
            high = jnp.where(slot_high[j], turned, high)
            if j == groups - 1 or u == len(units) - 1:
                pack_low[k, q] = low
                pack_high[k, q] = high
                low, high = zero, zero

    def prepare(g):
        place = unit_lane
        for j in range(1, groups):
            place = jnp.where(unit_lane >= HOP * j, unit_lane - HOP * j, place)
        place_low = place
        place_high = jnp.where(unit_lane >= width - HOP, unit_lane - (width - HOP), place)
        none = jnp.zeros((UNIT, width), jnp.int32)
        off_low, off_high, absorbed, emitted = none, none, zero, zero
        units = units_of(g)
        for u, (q, j, x, y) in enumerate(units):
            rows = pl.ds(y, UNIT)
            off = cell_off[x, rows]
            off_low = jnp.where(slot_low[j], off, off_low)
            off_high = jnp.where(slot_high[j], off, off_high)
            absorbed = jnp.where(slot_low[j], cell_absorb[x, rows], absorbed)
            emitted = jnp.where(slot_high[j], cell_emit[x, rows], emitted)
            if j == groups - 1 or u == len(units) - 1:
                from_low_at = unit_lane - off_low
                from_high_at = unit_lane + off_high
                turn_low[q] = jnp.where(from_low_at < 0, from_low_at + width, from_low_at)
                turn_high[q] = jnp.where(
                    from_high_at >= width, from_high_at - width, from_high_at
                )
                gain_low[q] = jnp.where(place_low < off_low, absorbed, 0.0)
                gain_high[q] = jnp.where(place_high >= HOP - off_high, emitted, 0.0)
                off_low, off_high, absorbed, emitted = none, none, zero, zero

    def unpack(k, g):
        def take(source, at, gain):
            return gain * jnp.take_along_axis(
                source, at, axis=1, mode="promise_in_bounds"
            )

        start, count = spans[g]
        low = [
            take(from_low[k, q], turn_low[q], gain_low[q])
            for q in range(start, start + count)
        ]
        high = [
            take(from_high[k, q], turn_high[q], gain_high[q])
            for q in range(start, start + count)
        ]
        for q, j, x, y in units_of(g):
            rows = pl.ds(y, UNIT)
            came = jnp.where(
                slot_low[j], low[q - start], jnp.where(slot_high[j], high[q - start], 0.0)
            )
            part[0, x, rows] = part[0, x, rows] + turn(came, -HOP * j)

    def first_plane(i, carry):
        x = plane_at(i)
        for y in range(0, ny, ROWS):
            rows = pl.ds(y, ROWS)
            diag = rate[x, rows] + 4.0 * diffusion
            px, py = cell_x[x, rows], cell_y[x, rows]
            inv_d = 1.0 / diag
            inv_t = 1.0 / (diag * diag + px * px + py * py)
            inv_diag[x, rows] = inv_d
            inv_det[x, rows] = inv_t
            r = [right[c, x, rows] for c in range(COEFS)]
            u = solve(r, px, py, diag, inv_d, inv_t)
            pinned = cell_pin[x, rows] == 1
            f = [jnp.where(pinned, r[c], u[c]) for c in range(COEFS)]
            for c in range(COEFS):
                field[0][c, x + 1, pl.ds(PAD + y, ROWS)] = f[c]
        return carry

    inner = pl.ds(PAD, ny)

    def to_right(k):
        return pltpu.make_async_remote_copy(
            src_ref=field[k].at[:, nx, inner],
            dst_ref=halo.at[k, 0],
            send_sem=x_send.at[k, 0],
            recv_sem=x_recv.at[k, 0],
            device_id=(e, s + 1),
            device_id_type=MESH,
        )

    def to_left(k):
        return pltpu.make_async_remote_copy(
            src_ref=field[k].at[:, 1, inner],
            dst_ref=halo.at[k, 1],
            send_sem=x_send.at[k, 1],
            recv_sem=x_recv.at[k, 1],
            device_id=(e, s - 1),
            device_id_type=MESH,
        )

    def to_upper(k, g):
        span = pl.ds(*spans[g])
        return pltpu.make_async_remote_copy(
            src_ref=pack_high.at[k, span],
            dst_ref=from_low.at[k, span],
            send_sem=e_send.at[k, g, 0],
            recv_sem=e_recv.at[k, g, 0],
            device_id=(e + 1, s),
            device_id_type=MESH,
        )

    def to_lower(k, g):
        span = pl.ds(*spans[g])
        return pltpu.make_async_remote_copy(
            src_ref=pack_low.at[k, span],
            dst_ref=from_high.at[k, span],
            send_sem=e_send.at[k, g, 1],
            recv_sem=e_recv.at[k, g, 1],
            device_id=(e - 1, s),
            device_id_type=MESH,
        )

    has_right, has_left = s < n_space - 1, s > 0
    has_upper, has_lower = e < n_energy - 1, e > 0

    def leave(k, g):
        if g == 0:

            @pl.when(has_right)
            def _():
                to_right(k).start()

            @pl.when(has_left)
            def _():
                to_left(k).start()

        @pl.when(has_upper)
        def _():
            to_upper(k, g).start()

        @pl.when(has_lower)
        def _():
            to_lower(k, g).start()

    def arrive(k, g):
        @pl.when(has_lower)
        def _():
            to_upper(k, g).wait_recv()

        @pl.when(has_upper)
        def _():
            to_lower(k, g).wait_recv()

    load_rate.wait()
    for g, (first, last) in enumerate(chunks):
        for load in load_right[first:last]:
            load.wait()
        lax.fori_loop(first, last, first_plane, 0)
        pack(0, g)
        if g == 0:
            pl.semaphore_wait(barrier, n_energy + n_space - 2)
        leave(0, g)
    for g in range(len(chunks)):
        prepare(g)
    for step in range(1, n_energy):
        pl.semaphore_signal(
            known,
            inc=1,
            device_id=(lax.rem(e + step, n_energy), s),
            device_id_type=MESH,
        )

    velocity = jnp.broadcast_to(0.5 * speed_ref[...], (ROWS, width))

    def inside_part(k):
        def plane(x, carry):
            for y in range(0, ny, ROWS):
                rows = pl.ds(y, ROWS)
                mid = pl.ds(PAD + y, ROWS)
                f = [field[k][c, x + 1, mid] for c in range(COEFS)]
                xp = [field[k][c, x + 2, mid] for c in range(COEFS)]
                xm = [field[k][c, x, mid] for c in range(COEFS)]
                yp = [field[k][c, x + 1, pl.ds(PAD + y + 1, ROWS)] for c in range(COEFS)]
                ym = [field[k][c, x + 1, pl.ds(PAD + y - 1, ROWS)] for c in range(COEFS)]
                diag = rate[x, rows] + 4.0 * diffusion
                px, py = cell_x[x, rows], cell_y[x, rows]
                nb = [xp[c] + xm[c] + (yp[c] + ym[c]) for c in range(COEFS)]
                below, above = rotated(f[0], cell_off[x, rows])
                image = [
                    diag * f[0]
                    + px * f[1]
                    + py * f[2]
                    - diffusion * nb[0]
                    + velocity * (xp[1] - xm[1] + (yp[2] - ym[2]))
                    - (cell_absorb[x, rows] * below + cell_emit[x, rows] * above),
                    diag * f[1] - px * f[0] - diffusion * nb[1] + velocity * (xp[0] - xm[0]),
                    diag * f[2] - py * f[0] - diffusion * nb[2] + velocity * (yp[0] - ym[0]),
                    diag * f[3] - diffusion * nb[3],
                ]
                pinned = cell_pin[x, rows] == 1
                for c in range(COEFS):
                    part[c, x, rows] = right[c, x, rows] - jnp.where(pinned, f[c], image[c])
            return carry

        lax.fori_loop(0, nx, plane, 0)

    def beside_part(k):
        def side(where, x, sign):
            for y in range(0, ny, ROWS):
                rows = pl.ds(y, ROWS)
                h = [halo[k, where, c, rows] for c in range(COEFS)]
                free = cell_pin[x, rows] != 1
                swing = sign * velocity
                gain = [
                    diffusion * h[0] - swing * h[1],
                    diffusion * h[1] - swing * h[0],
                    diffusion * h[2],
                    diffusion * h[3],
                ]
                for c in range(COEFS):
                    part[c, x, rows] = part[c, x, rows] + jnp.where(free, gain[c], 0.0)

        @pl.when(has_left)
        def _():
            to_right(k).wait_recv()
            side(0, 0, -1.0)

        @pl.when(has_right)
        def _():
            to_left(k).wait_recv()
            side(1, nx - 1, 1.0)

    def folded(value):
        square = value * value
        out = square[0:UNIT]
        for i in range(UNIT, ROWS, UNIT):
            out = out + square[i : i + UNIT]
        return out

    def outside_plane(k):
        def plane(i, carry):
            x = plane_at(i)
            acc = list(carry)
            for y in range(0, ny, ROWS):
                rows = pl.ds(y, ROWS)
                r = [part[c, x, rows] for c in range(COEFS)]
                for c in range(COEFS):
                    acc[c] = acc[c] + folded(r[c])
                if k < SWEEPS - 1:
                    diag = rate[x, rows] + 4.0 * diffusion
                    px, py = cell_x[x, rows], cell_y[x, rows]
                    u = solve(r, px, py, diag, inv_diag[x, rows], inv_det[x, rows])
                    pinned = cell_pin[x, rows] == 1
                    mid = pl.ds(PAD + y, ROWS)
                    f = [
                        field[k][c, x + 1, mid] + jnp.where(pinned, r[c], u[c])
                        for c in range(COEFS)
                    ]
                    for c in range(COEFS):
                        field[k + 1][c, x + 1, mid] = f[c]
            return tuple(acc)

        return plane

    spot = lax.broadcasted_iota(jnp.int32, (SWEEPS * COEFS, width), 0)
    mine = jnp.zeros((SWEEPS * COEFS, width), jnp.float32)
    store = pltpu.make_async_copy(
        field[SWEEPS - 1].at[:, pl.ds(1, nx), inner], state_ref, out_sem
    )
    for k in range(SWEEPS):
        if k == SWEEPS - 1:
            store.start()
        inside_part(k)
        beside_part(k)
        acc = (zero,) * COEFS
        for g, (first, last) in enumerate(chunks):
            arrive(k, g)
            unpack(k, g)
            acc = lax.fori_loop(first, last, outside_plane(k), acc)
            if k < SWEEPS - 1:
                pack(k + 1, g)
                leave(k + 1, g)
        for c, value in enumerate(acc):
            mine = jnp.where(
                spot == COEFS * k + c, jnp.sum(value, axis=0, keepdims=True), mine
            )

    sums[me] = mine
    pl.semaphore_wait(known, n_energy - 1)

    def tell(to_e, to_s, rows):
        return pltpu.make_async_remote_copy(
            src_ref=sums.at[rows],
            dst_ref=sums.at[rows],
            send_sem=n_send,
            recv_sem=n_recv,
            device_id=(to_e, to_s),
            device_id_type=MESH,
        )

    def others_of(at, size):
        out = []
        for i in range(size - 1):
            down, up = size - 1 - i, i
            down = jnp.where(down > at, down, down - 1)
            up = jnp.where(up < at, up, up + 1)
            out.append(jnp.where(at < size // 2, down, up))
        return out

    own = pl.ds(me, 1)
    for to_s in others_of(s, n_space):
        for i in range(n_energy):
            tell(jnp.where(e < n_energy // 2, n_energy - 1 - i, i), to_s, own).start()
    for to_e in others_of(e, n_energy):
        tell(to_e, s, own).start()
    for k in range(SWEEPS):

        @pl.when(has_right)
        def _():
            to_right(k).wait_send()

        @pl.when(has_left)
        def _():
            to_left(k).wait_send()

        for g in range(len(chunks)):

            @pl.when(has_upper)
            def _():
                to_upper(k, g).wait_send()

            @pl.when(has_lower)
            def _():
                to_lower(k, g).wait_send()

    store.wait()
    others = tell(e, lax.rem(s + 1, n_space), pl.ds(0, n_energy * n_space - 1))
    others.wait_recv()
    others.wait_send()
    sums_ref[...] = jnp.sum(sums[...], axis=0)


def finish(state, sums_ref, state_hbm, norms_hbm, norms, sem):
    stores = [
        pltpu.make_async_copy(state.at[c], state_hbm.at[c], sem.at[c]) for c in range(COEFS)
    ]
    for store in stores:
        store.start()
    shape = sums_ref.shape
    norm = jnp.broadcast_to(
        jnp.sqrt(jnp.sum(sums_ref[...], axis=1, keepdims=True)), shape
    )
    row = lax.broadcasted_iota(jnp.int32, shape, 0)
    lane = lax.broadcasted_iota(jnp.int32, shape, 1)
    for k in range(SWEEPS):
        line = jnp.sum(
            jnp.where(row == lane + COEFS * k, norm, 0.0), axis=0, keepdims=True
        )
        norms[k : k + 1, :] = line[:, 0:COEFS]
    store = pltpu.make_async_copy(norms, norms_hbm, sem.at[COEFS])
    store.start()
    for load in (*stores, store):
        load.wait()


def chunks_of(nx):
    edge = min(2, nx)
    cuts = [0, edge, edge + (nx - edge) // 2, nx]
    return [(a, b) for a, b in zip(cuts[:-1], cuts[1:]) if b > a]


def spans_of(chunks, tall, groups):
    out, start = [], 0
    for first, last in chunks:
        count = -(-(last - first) * tall // groups)
        out.append((start, count))
        start += count
    return out


def solution(mesh):
    n_energy, n_space = mesh.shape["energy"], mesh.shape["space"]

    def local(right_side, rate, fields, speed, regions, contacts, offsets, phonon):
        coefs, nx, ny, width = right_side.shape
        spans = spans_of(chunks_of(nx), ny // UNIT, width // HOP)
        chunks, packs = len(spans), sum(spans[-1])
        plane = (nx, ny, width)
        vmem = pl.BlockSpec(memory_space=pltpu.VMEM)
        hbm = pl.BlockSpec(memory_space=pl.ANY)
        f32 = jnp.float32
        pack = pltpu.VMEM((SWEEPS, packs, UNIT, width), f32)
        lines = SWEEPS * coefs
        state, sums = pl.pallas_call(
            functools.partial(kernel, n_energy, n_space),
            out_shape=(
                pltpu.VMEM(right_side.shape, f32),
                pltpu.VMEM((lines, width), f32),
            ),
            in_specs=[pl.BlockSpec(memory_space=pltpu.HBM)] * 8,
            out_specs=(vmem, vmem),
            scratch_shapes=[
                pltpu.SMEM(offsets.shape, offsets.dtype),
                pltpu.SMEM((phonon.shape[1], phonon.shape[0]), f32),
                pltpu.VMEM(fields.shape, f32),
                pltpu.VMEM((1, width), f32),
                pltpu.VMEM(regions.shape, regions.dtype),
                pltpu.VMEM(contacts.shape, contacts.dtype),
                pltpu.VMEM(right_side.shape, f32),
                pltpu.VMEM(plane, f32),
                pltpu.VMEM((coefs, nx + 2, ny + 2 * PAD, width), f32),
                pltpu.VMEM((coefs, nx + 2, ny + 2 * PAD, width), f32),
                pltpu.VMEM(right_side.shape, f32),
                pltpu.VMEM((SWEEPS, 2, coefs, ny, width), f32),
                pltpu.VMEM(plane, f32),
                pltpu.VMEM(plane, f32),
                pltpu.VMEM(plane, jnp.int32),
                pltpu.VMEM(plane, jnp.int32),
                pltpu.VMEM(plane, f32),
                pltpu.VMEM(plane, f32),
                pltpu.VMEM(plane, f32),
                pltpu.VMEM(plane, f32),
                pltpu.VMEM((packs, UNIT, width), jnp.int32),
                pltpu.VMEM((packs, UNIT, width), jnp.int32),
                pltpu.VMEM((packs, UNIT, width), f32),
                pltpu.VMEM((packs, UNIT, width), f32),
                pack,
                pack,
                pack,
                pack,
                pltpu.VMEM((n_energy * n_space, lines, width), f32),
                pltpu.SemaphoreType.DMA((7 + nx,)),
                pltpu.SemaphoreType.DMA,
                pltpu.SemaphoreType.DMA((SWEEPS, 2)),
                pltpu.SemaphoreType.DMA((SWEEPS, 2)),
                pltpu.SemaphoreType.DMA((SWEEPS, chunks, 2)),
                pltpu.SemaphoreType.DMA((SWEEPS, chunks, 2)),
                pltpu.SemaphoreType.DMA,
                pltpu.SemaphoreType.DMA,
                pltpu.SemaphoreType.REGULAR,
            ],
            compiler_params=pltpu.CompilerParams(
                collective_id=0, has_side_effects=True, vmem_limit_bytes=24 << 20
            ),
        )(
            *(
                pltpu.with_memory_space_constraint(value, pltpu.HBM)
                for value in (
                    offsets,
                    phonon.T,
                    right_side,
                    rate,
                    fields,
                    speed.reshape(1, width),
                    regions,
                    contacts,
                )
            )
        )
        return pl.pallas_call(
            finish,
            out_shape=(
                jax.ShapeDtypeStruct(right_side.shape, f32),
                jax.ShapeDtypeStruct((SWEEPS, coefs), f32),
            ),
            in_specs=[vmem, vmem],
            out_specs=(hbm, hbm),
            scratch_shapes=[
                pltpu.VMEM((SWEEPS, coefs), f32),
                pltpu.SemaphoreType.DMA((coefs + 1,)),
            ],
            compiler_params=pltpu.CompilerParams(vmem_limit_bytes=8 << 20),
        )(state, sums)

    in_specs = (
        P(None, "space", None, "energy"),
        P("space", None, "energy"),
        P(None, "space", None),
        P("energy"),
        P("space", None),
        P("space", None),
        P(),
        P(),
    )
    out_specs = (P(None, "space", None, "energy"), P())
    return jax.shard_map(local, mesh=mesh, in_specs=in_specs, out_specs=out_specs, check_vma=False)
```

```python
import functools

import jax
import jax.numpy as jnp
from jax import lax
from jax.experimental import pallas as pl
from jax.experimental.pallas import tpu as pltpu
from jax.sharding import PartitionSpec as P

HOP = 24
REGIONS = 4
SWEEPS = 2
COEFS = 4
PAD = 8
ROWS = 16
UNIT = 8

diffusion = 0.25

MESH = pl.DeviceIdType.MESH


def kernel(
    n_energy,
    n_space,
    offsets_hbm,
    phonon_hbm,
    right_hbm,
    rate_hbm,
    fields_hbm,
    speed_hbm,
    regions_hbm,
    contacts_hbm,
    state_ref,
    sums_ref,
    offsets_ref,
    phonon_ref,
    fields_ref,
    speed_ref,
    regions_ref,
    contacts_ref,
    right,
    rate,
    field_0,
    field_1,
    part,
    halo,
    cell_x,
    cell_y,
    cell_pin,
    cell_off,
    cell_absorb,
    cell_emit,
    inv_diag,
    inv_det,
    turn_low,
    turn_high,
    gain_low,
    gain_high,
    pack_low,
    pack_high,
    from_low,
    from_high,
    sums,
    in_sem,
    out_sem,
    x_send,
    x_recv,
    e_send,
    e_recv,
    n_send,
    n_recv,
    known,
):
    nx, ny, width = right.shape[1:]
    groups = width // HOP
    tall = ny // UNIT
    field = (field_0, field_1)
    chunks = chunks_of(nx)
    spans = spans_of(chunks, tall, groups)
    e = lax.axis_index("energy")
    s = lax.axis_index("space")
    me = e * n_space + s

    def greet(semaphore, step):
        @pl.when(s >= step)
        def _():
            pl.semaphore_signal(
                semaphore, inc=1, device_id=(e, s - step), device_id_type=MESH
            )

        @pl.when(s + step < n_space)
        def _():
            pl.semaphore_signal(
                semaphore, inc=1, device_id=(e, s + step), device_id_type=MESH
            )

    def greeted(step):
        return (s >= step).astype(jnp.int32) + (s + step < n_space).astype(jnp.int32)

    steps = steps_of(n_space)

    def hear(i):
        pl.semaphore_wait(known.at[i], greeted(steps[i]))
        if i + 1 < len(steps):
            greet(known.at[i + 1], steps[i + 1])

    barrier = pltpu.get_barrier_semaphore()
    def plane_at(i):
        turned, step = lax.rem(i, 2), lax.div(i, 2)
        return step + turned * (nx - 1 - 2 * step)

    def plane_of(i):
        return i // 2 if i % 2 == 0 else nx - 1 - i // 2

    copies = [
        *((right_hbm.at[:, plane_of(i)], right.at[:, plane_of(i)]) for i in range(nx)),
        (rate_hbm, rate),
        (fields_hbm, fields_ref),
        (contacts_hbm, contacts_ref),
        (offsets_hbm, offsets_ref),
        (phonon_hbm, phonon_ref),
        (regions_hbm, regions_ref),
        (speed_hbm, speed_ref),
    ]
    loads = [
        pltpu.make_async_copy(source, target, in_sem.at[i])
        for i, (source, target) in enumerate(copies)
    ]
    load_right, load_rate = loads[:nx], loads[nx]
    cells, small = loads[nx + 1 : nx + 3], loads[nx + 3 :]
    for load in (*cells, load_rate, *load_right, *small):
        load.start()

    for step in range(1, n_energy):
        pl.semaphore_signal(
            barrier,
            inc=1,
            device_id=(lax.rem(e + step, n_energy), s),
            device_id_type=MESH,
        )
    greet(barrier, 1)

    zero_rows = jnp.zeros((PAD, width), jnp.float32)
    zero_plane = jnp.zeros((ny, width), jnp.float32)
    for k in range(SWEEPS):
        for c in range(COEFS):
            for x in range(1, nx + 1):
                field[k][c, x, 0:PAD] = zero_rows
                field[k][c, x, PAD + ny : 2 * PAD + ny] = zero_rows
            field[k][c, 0, PAD : PAD + ny] = zero_plane
            field[k][c, nx + 1, PAD : PAD + ny] = zero_plane

    @pl.when(e == 0)
    def _():
        for k in range(SWEEPS):
            from_low[k] = jnp.zeros(from_low.shape[1:], jnp.float32)

    @pl.when(e == n_energy - 1)
    def _():
        for k in range(SWEEPS):
            from_high[k] = jnp.zeros(from_high.shape[1:], jnp.float32)

    def spread(*pairs):
        for source, target in pairs:
            turned = source.T
            for x in range(nx):
                target[x] = jnp.broadcast_to(turned[:, x : x + 1], (ny, width))

    for load in cells:
        load.wait()
    spread((fields_ref[0], cell_x), (fields_ref[1], cell_y), (contacts_ref[...], cell_pin))

    def solve(r, px, py, diag, inv_d, inv_t):
        first = (diag * r[0] - px * r[1] - py * r[2]) * inv_t
        return (
            first,
            (r[1] + px * first) * inv_d,
            (r[2] + py * first) * inv_d,
            r[3] * inv_d,
        )

    lane = lax.broadcasted_iota(jnp.int32, (ROWS, width), 1)
    unit_lane = lax.broadcasted_iota(jnp.int32, (UNIT, width), 1)

    def slot(at):
        at = at % width
        return (unit_lane >= at) & (unit_lane < at + HOP)

    slot_low = [slot(HOP * j) for j in range(groups)]
    slot_high = [slot(HOP * (j - 1)) for j in range(groups)]
    zero = jnp.zeros((UNIT, width), jnp.float32)

    def turn(value, by):
        by = by % width
        return pltpu.roll(value, by, 1) if by else value

    def units_of(g):
        first, last = chunks[g]
        units = [(plane_of(i), y) for i in range(first, last) for y in range(0, ny, UNIT)]
        start = spans[g][0]
        return [(start + u // groups, u % groups, *unit) for u, unit in enumerate(units)]

    def rotated(f, off):
        low, high = lane < off, lane >= width - off
        below = jnp.take_along_axis(
            f,
            jnp.where(low, lane - off + width, lane - off),
            axis=1,
            mode="promise_in_bounds",
        )
        above = jnp.take_along_axis(
            f,
            jnp.where(high, lane + off - width, lane + off),
            axis=1,
            mode="promise_in_bounds",
        )
        return jnp.where(low, 0.0, below), jnp.where(high, 0.0, above)

    def pack(k, g):
        low, high = zero, zero
        units = units_of(g)
        for u, (q, j, x, y) in enumerate(units):
            turned = turn(field[k][0, x + 1, pl.ds(PAD + y, UNIT)], HOP * j)
            low = jnp.where(slot_low[j], turned, low)
            high = jnp.where(slot_high[j], turned, high)
            if j == groups - 1 or u == len(units) - 1:
                pack_low[k, q] = low
                pack_high[k, q] = high
                low, high = zero, zero

    def prepare(g):
        place = unit_lane
        for j in range(1, groups):
            place = jnp.where(unit_lane >= HOP * j, unit_lane - HOP * j, place)
        place_low = place
        place_high = jnp.where(unit_lane >= width - HOP, unit_lane - (width - HOP), place)
        none = jnp.zeros((UNIT, width), jnp.int32)
        off_low, off_high, absorbed, emitted = none, none, zero, zero
        units = units_of(g)
        for u, (q, j, x, y) in enumerate(units):
            rows = pl.ds(y, UNIT)
            off = cell_off[x, rows]
            off_low = jnp.where(slot_low[j], off, off_low)
            off_high = jnp.where(slot_high[j], off, off_high)
            absorbed = jnp.where(slot_low[j], cell_absorb[x, rows], absorbed)
            emitted = jnp.where(slot_high[j], cell_emit[x, rows], emitted)
            if j == groups - 1 or u == len(units) - 1:
                from_low_at = unit_lane - off_low
                from_high_at = unit_lane + off_high
                turn_low[q] = jnp.where(from_low_at < 0, from_low_at + width, from_low_at)
                turn_high[q] = jnp.where(
                    from_high_at >= width, from_high_at - width, from_high_at
                )
                gain_low[q] = jnp.where(place_low < off_low, absorbed, 0.0)
                gain_high[q] = jnp.where(place_high >= HOP - off_high, emitted, 0.0)
                off_low, off_high, absorbed, emitted = none, none, zero, zero

    def first_plane(i, carry):
        x = plane_at(i)
        for y in range(0, ny, ROWS):
            rows = pl.ds(y, ROWS)
            diag = rate[x, rows] + 4.0 * diffusion
            px, py = cell_x[x, rows], cell_y[x, rows]
            inv_d = 1.0 / diag
            inv_t = 1.0 / (diag * diag + px * px + py * py)
            inv_diag[x, rows] = inv_d
            inv_det[x, rows] = inv_t
            r = [right[c, x, rows] for c in range(COEFS)]
            u = solve(r, px, py, diag, inv_d, inv_t)
            pinned = cell_pin[x, rows] == 1
            f = [jnp.where(pinned, r[c], u[c]) for c in range(COEFS)]
            for c in range(COEFS):
                field[0][c, x + 1, pl.ds(PAD + y, ROWS)] = f[c]
        return carry

    inner = pl.ds(PAD, ny)

    def to_right(k):
        return pltpu.make_async_remote_copy(
            src_ref=field[k].at[:, nx, inner],
            dst_ref=halo.at[k, 0],
            send_sem=x_send.at[k, 0],
            recv_sem=x_recv.at[k, 0],
            device_id=(e, s + 1),
            device_id_type=MESH,
        )

    def to_left(k):
        return pltpu.make_async_remote_copy(
            src_ref=field[k].at[:, 1, inner],
            dst_ref=halo.at[k, 1],
            send_sem=x_send.at[k, 1],
            recv_sem=x_recv.at[k, 1],
            device_id=(e, s - 1),
            device_id_type=MESH,
        )

    def to_upper(k, g):
        span = pl.ds(*spans[g])
        return pltpu.make_async_remote_copy(
            src_ref=pack_high.at[k, span],
            dst_ref=from_low.at[k, span],
            send_sem=e_send.at[k, g, 0],
            recv_sem=e_recv.at[k, g, 0],
            device_id=(e + 1, s),
            device_id_type=MESH,
        )

    def to_lower(k, g):
        span = pl.ds(*spans[g])
        return pltpu.make_async_remote_copy(
            src_ref=pack_low.at[k, span],
            dst_ref=from_high.at[k, span],
            send_sem=e_send.at[k, g, 1],
            recv_sem=e_recv.at[k, g, 1],
            device_id=(e - 1, s),
            device_id_type=MESH,
        )

    has_right, has_left = s < n_space - 1, s > 0
    has_upper, has_lower = e < n_energy - 1, e > 0

    def leave_sides(k):
        @pl.when(has_right)
        def _():
            to_right(k).start()

        @pl.when(has_left)
        def _():
            to_left(k).start()

    def leave(k, g):
        @pl.when(has_upper)
        def _():
            to_upper(k, g).start()

        @pl.when(has_lower)
        def _():
            to_lower(k, g).start()

    def arrive(k, g):
        @pl.when(has_lower)
        def _():
            to_upper(k, g).wait_recv()

        @pl.when(has_upper)
        def _():
            to_lower(k, g).wait_recv()

    load_rate.wait()
    for g, (first, last) in enumerate(chunks):
        for load in load_right[first:last]:
            load.wait()
        lax.fori_loop(first, last, first_plane, 0)
        if g == 0:
            pl.semaphore_wait(barrier, n_energy - 1 + greeted(1))
            leave_sides(0)
        pack(0, g)
        leave(0, g)
    greet(known.at[0], steps[0])
    for load in small:
        load.wait()
    region = regions_ref[...]
    free = contacts_ref[...] != 1
    off = jnp.zeros_like(region)
    absorb = jnp.zeros(region.shape, jnp.float32)
    emit = jnp.zeros(region.shape, jnp.float32)
    for r in range(REGIONS):
        inside = region == r
        off = jnp.where(inside, offsets_ref[r], off)
        absorb = jnp.where(inside & free, phonon_ref[0, r], absorb)
        emit = jnp.where(inside & free, phonon_ref[1, r], emit)
    spread((off, cell_off), (absorb, cell_absorb), (emit, cell_emit))
    for g in range(len(chunks)):
        prepare(g)
    velocity = jnp.broadcast_to(0.5 * speed_ref[...], (ROWS, width))

    def inside_part(k):
        def plane(x, carry):
            for y in range(0, ny, ROWS):
                rows = pl.ds(y, ROWS)
                mid = pl.ds(PAD + y, ROWS)
                f = [field[k][c, x + 1, mid] for c in range(COEFS)]
                xp = [field[k][c, x + 2, mid] for c in range(COEFS)]
                xm = [field[k][c, x, mid] for c in range(COEFS)]
                yp = [field[k][c, x + 1, pl.ds(PAD + y + 1, ROWS)] for c in range(COEFS)]
                ym = [field[k][c, x + 1, pl.ds(PAD + y - 1, ROWS)] for c in range(COEFS)]
                diag = rate[x, rows] + 4.0 * diffusion
                px, py = cell_x[x, rows], cell_y[x, rows]
                nb = [xp[c] + xm[c] + (yp[c] + ym[c]) for c in range(COEFS)]
                below, above = rotated(f[0], cell_off[x, rows])
                image = [
                    diag * f[0]
                    + px * f[1]
                    + py * f[2]
                    - diffusion * nb[0]
                    + velocity * (xp[1] - xm[1] + (yp[2] - ym[2]))
                    - (cell_absorb[x, rows] * below + cell_emit[x, rows] * above),
                    diag * f[1] - px * f[0] - diffusion * nb[1] + velocity * (xp[0] - xm[0]),
                    diag * f[2] - py * f[0] - diffusion * nb[2] + velocity * (yp[0] - ym[0]),
                    diag * f[3] - diffusion * nb[3],
                ]
                pinned = cell_pin[x, rows] == 1
                for c in range(COEFS):
                    part[c, x, rows] = right[c, x, rows] - jnp.where(pinned, f[c], image[c])
            return carry

        lax.fori_loop(0, nx, plane, 0)

    def beside_part(k):
        def side(where, x, sign):
            for y in range(0, ny, ROWS):
                rows = pl.ds(y, ROWS)
                h = [halo[k, where, c, rows] for c in range(COEFS)]
                free = cell_pin[x, rows] != 1
                swing = sign * velocity
                gain = [
                    diffusion * h[0] - swing * h[1],
                    diffusion * h[1] - swing * h[0],
                    diffusion * h[2],
                    diffusion * h[3],
                ]
                for c in range(COEFS):
                    part[c, x, rows] = part[c, x, rows] + jnp.where(free, gain[c], 0.0)

        @pl.when(has_left)
        def _():
            to_right(k).wait_recv()
            side(0, 0, -1.0)

        @pl.when(has_right)
        def _():
            to_left(k).wait_recv()
            side(1, nx - 1, 1.0)

    def outside_part(k, g, acc):
        def take(source, at, gain):
            return gain * jnp.take_along_axis(
                source, at, axis=1, mode="promise_in_bounds"
            )

        start, count = spans[g]
        here = range(start, start + count)
        low = [take(from_low[k, q], turn_low[q], gain_low[q]) for q in here]
        high = [take(from_high[k, q], turn_high[q], gain_high[q]) for q in here]
        acc = list(acc)
        for q, j, x, y in units_of(g):
            rows, mid = pl.ds(y, UNIT), pl.ds(PAD + y, UNIT)
            came = jnp.where(
                slot_low[j], low[q - start], jnp.where(slot_high[j], high[q - start], 0.0)
            )
            r = [part[c, x, rows] for c in range(COEFS)]
            r[0] = r[0] + turn(came, -HOP * j)
            for c in range(COEFS):
                acc[c] = acc[c] + r[c] * r[c]
            if k < SWEEPS - 1:
                diag = rate[x, rows] + 4.0 * diffusion
                px, py = cell_x[x, rows], cell_y[x, rows]
                u = solve(r, px, py, diag, inv_diag[x, rows], inv_det[x, rows])
                pinned = cell_pin[x, rows] == 1
                for c in range(COEFS):
                    field[k + 1][c, x + 1, mid] = field[k][c, x + 1, mid] + jnp.where(
                        pinned, r[c], u[c]
                    )
        return tuple(acc)

    spot = lax.broadcasted_iota(jnp.int32, (SWEEPS * COEFS, width), 0)
    mine = jnp.zeros((SWEEPS * COEFS, width), jnp.float32)
    store = pltpu.make_async_copy(
        field[SWEEPS - 1].at[:, pl.ds(1, nx), inner], state_ref, out_sem
    )
    for k in range(SWEEPS):
        if k == SWEEPS - 1:
            store.start()
        inside_part(k)
        if 0 < k < len(steps):
            hear(k)
        beside_part(k)
        if k == 0:
            hear(0)
        acc = (zero,) * COEFS
        for g in range(len(chunks)):
            arrive(k, g)
            acc = outside_part(k, g, acc)
            if k < SWEEPS - 1:
                if g == 0:
                    leave_sides(k + 1)
                pack(k + 1, g)
                leave(k + 1, g)
        for c, value in enumerate(acc):
            mine = jnp.where(
                spot == COEFS * k + c, jnp.sum(value, axis=0, keepdims=True), mine
            )

    lines = SWEEPS * COEFS
    share = width // lines
    by = width // 2
    while by >= share:
        mine = mine + pltpu.roll(mine, by, 1)
        by //= 2
    at = lax.broadcasted_iota(jnp.int32, (lines, width), 1)
    own_lanes = (at >= spot * share) & (at < (spot + 1) * share)
    sums[me] = jnp.sum(jnp.where(own_lanes, mine, 0.0), axis=0, keepdims=True)
    for i in range(SWEEPS, len(steps)):
        hear(i)

    def tell(to_e, to_s, rows):
        return pltpu.make_async_remote_copy(
            src_ref=sums.at[rows],
            dst_ref=sums.at[rows],
            send_sem=n_send,
            recv_sem=n_recv,
            device_id=(to_e, to_s),
            device_id_type=MESH,
        )

    def others_of(at, size):
        out = []
        for i in range(size - 1):
            down, up = size - 1 - i, i
            down = jnp.where(down > at, down, down - 1)
            up = jnp.where(up < at, up, up + 1)
            out.append(jnp.where(at < size // 2, down, up))
        return out

    own = pl.ds(me, 1)
    for to_s in others_of(s, n_space):
        for i in range(n_energy):
            tell(jnp.where(e < n_energy // 2, n_energy - 1 - i, i), to_s, own).start()
    for to_e in others_of(e, n_energy):
        tell(to_e, s, own).start()
    for k in range(SWEEPS):

        @pl.when(has_right)
        def _():
            to_right(k).wait_send()

        @pl.when(has_left)
        def _():
            to_left(k).wait_send()

        for g in range(len(chunks)):

            @pl.when(has_upper)
            def _():
                to_upper(k, g).wait_send()

            @pl.when(has_lower)
            def _():
                to_lower(k, g).wait_send()

    store.wait()
    others = tell(e, lax.rem(s + 1, n_space), pl.ds(0, n_energy * n_space - 1))
    others.wait_recv()
    others.wait_send()
    sums_ref[...] = jnp.sum(sums[...], axis=0)


def finish(state, sums_ref, state_hbm, norms_hbm, norms, sem):
    stores = [
        pltpu.make_async_copy(state.at[c], state_hbm.at[c], sem.at[c]) for c in range(COEFS)
    ]
    for store in stores:
        store.start()
    width = sums_ref.shape[1]
    lines = SWEEPS * COEFS
    share = width // lines
    shape = (lines, width)
    row = lax.broadcasted_iota(jnp.int32, shape, 0)
    lane = lax.broadcasted_iota(jnp.int32, shape, 1)
    own_lanes = (lane >= row * share) & (lane < (row + 1) * share)
    spread = jnp.where(own_lanes, jnp.broadcast_to(sums_ref[...], shape), 0.0)
    norm = jnp.broadcast_to(jnp.sqrt(jnp.sum(spread, axis=1, keepdims=True)), shape)
    for k in range(SWEEPS):
        line = jnp.sum(
            jnp.where(row == lane + COEFS * k, norm, 0.0), axis=0, keepdims=True
        )
        norms[k : k + 1, :] = line[:, 0:COEFS]
    store = pltpu.make_async_copy(norms, norms_hbm, sem.at[COEFS])
    store.start()
    for load in (*stores, store):
        load.wait()


def steps_of(n_space):
    steps = [1]
    while 2 * steps[-1] < n_space:
        steps.append(2 * steps[-1])
    return steps


def chunks_of(nx):
    edge = min(2, nx)
    cuts = [0, edge, edge + (nx - edge) // 2, nx]
    return [(a, b) for a, b in zip(cuts[:-1], cuts[1:]) if b > a]


def spans_of(chunks, tall, groups):
    out, start = [], 0
    for first, last in chunks:
        count = -(-(last - first) * tall // groups)
        out.append((start, count))
        start += count
    return out


def solution(mesh):
    n_energy, n_space = mesh.shape["energy"], mesh.shape["space"]

    def local(right_side, rate, fields, speed, regions, contacts, offsets, phonon):
        coefs, nx, ny, width = right_side.shape
        spans = spans_of(chunks_of(nx), ny // UNIT, width // HOP)
        chunks, packs = len(spans), sum(spans[-1])
        plane = (nx, ny, width)
        vmem = pl.BlockSpec(memory_space=pltpu.VMEM)
        hbm = pl.BlockSpec(memory_space=pl.ANY)
        f32 = jnp.float32
        pack = pltpu.VMEM((SWEEPS, packs, UNIT, width), f32)
        state, sums = pl.pallas_call(
            functools.partial(kernel, n_energy, n_space),
            out_shape=(
                pltpu.VMEM(right_side.shape, f32),
                pltpu.VMEM((1, width), f32),
            ),
            in_specs=[pl.BlockSpec(memory_space=pltpu.HBM)] * 8,
            out_specs=(vmem, vmem),
            scratch_shapes=[
                pltpu.SMEM(offsets.shape, offsets.dtype),
                pltpu.SMEM((phonon.shape[1], phonon.shape[0]), f32),
                pltpu.VMEM(fields.shape, f32),
                pltpu.VMEM((1, width), f32),
                pltpu.VMEM(regions.shape, regions.dtype),
                pltpu.VMEM(contacts.shape, contacts.dtype),
                pltpu.VMEM(right_side.shape, f32),
                pltpu.VMEM(plane, f32),
                pltpu.VMEM((coefs, nx + 2, ny + 2 * PAD, width), f32),
                pltpu.VMEM((coefs, nx + 2, ny + 2 * PAD, width), f32),
                pltpu.VMEM(right_side.shape, f32),
                pltpu.VMEM((SWEEPS, 2, coefs, ny, width), f32),
                pltpu.VMEM(plane, f32),
                pltpu.VMEM(plane, f32),
                pltpu.VMEM(plane, jnp.int32),
                pltpu.VMEM(plane, jnp.int32),
                pltpu.VMEM(plane, f32),
                pltpu.VMEM(plane, f32),
                pltpu.VMEM(plane, f32),
                pltpu.VMEM(plane, f32),
                pltpu.VMEM((packs, UNIT, width), jnp.int32),
                pltpu.VMEM((packs, UNIT, width), jnp.int32),
                pltpu.VMEM((packs, UNIT, width), f32),
                pltpu.VMEM((packs, UNIT, width), f32),
                pack,
                pack,
                pack,
                pack,
                pltpu.VMEM((n_energy * n_space, 1, width), f32),
                pltpu.SemaphoreType.DMA((7 + nx,)),
                pltpu.SemaphoreType.DMA,
                pltpu.SemaphoreType.DMA((SWEEPS, 2)),
                pltpu.SemaphoreType.DMA((SWEEPS, 2)),
                pltpu.SemaphoreType.DMA((SWEEPS, chunks, 2)),
                pltpu.SemaphoreType.DMA((SWEEPS, chunks, 2)),
                pltpu.SemaphoreType.DMA,
                pltpu.SemaphoreType.DMA,
                pltpu.SemaphoreType.REGULAR((len(steps_of(n_space)),)),
            ],
            compiler_params=pltpu.CompilerParams(
                collective_id=0, has_side_effects=True, vmem_limit_bytes=24 << 20
            ),
        )(
            *(
                pltpu.with_memory_space_constraint(value, pltpu.HBM)
                for value in (
                    offsets,
                    phonon.T,
                    right_side,
                    rate,
                    fields,
                    speed.reshape(1, width),
                    regions,
                    contacts,
                )
            )
        )
        return pl.pallas_call(
            finish,
            out_shape=(
                jax.ShapeDtypeStruct(right_side.shape, f32),
                jax.ShapeDtypeStruct((SWEEPS, coefs), f32),
            ),
            in_specs=[vmem, vmem],
            out_specs=(hbm, hbm),
            scratch_shapes=[
                pltpu.VMEM((SWEEPS, coefs), f32),
                pltpu.SemaphoreType.DMA((coefs + 1,)),
            ],
            compiler_params=pltpu.CompilerParams(vmem_limit_bytes=8 << 20),
        )(state, sums)

    in_specs = (
        P(None, "space", None, "energy"),
        P("space", None, "energy"),
        P(None, "space", None),
        P("energy"),
        P("space", None),
        P("space", None),
        P(),
        P(),
    )
    out_specs = (P(None, "space", None, "energy"), P())
    return jax.shard_map(local, mesh=mesh, in_specs=in_specs, out_specs=out_specs, check_vma=False)
```

```python
import functools

import jax
import jax.numpy as jnp
from jax import lax
from jax.experimental import pallas as pl
from jax.experimental.pallas import tpu as pltpu
from jax.sharding import PartitionSpec as P

HOP = 24
REGIONS = 4
SWEEPS = 2
COEFS = 4
MAIN = 3
PAD = 8
ROWS = 16
UNIT = 8

diffusion = 0.25

MESH = pl.DeviceIdType.MESH


def kernel(
    n_energy,
    n_space,
    offsets_hbm,
    phonon_hbm,
    right_hbm,
    rate_hbm,
    fields_hbm,
    speed_hbm,
    regions_hbm,
    contacts_hbm,
    state_ref,
    sums_ref,
    offsets_ref,
    phonon_ref,
    fields_ref,
    speed_ref,
    regions_ref,
    contacts_ref,
    right,
    rate,
    field_0,
    field_1,
    part,
    halo,
    cell_x,
    cell_y,
    cell_pin,
    cell_off,
    cell_absorb,
    cell_emit,
    inv_diag,
    inv_det,
    turn_low,
    turn_high,
    gain_low,
    gain_high,
    pack_low,
    pack_high,
    from_low,
    from_high,
    sums,
    in_sem,
    out_sem,
    x_send,
    x_recv,
    e_send,
    e_recv,
    n_send,
    n_recv,
    known,
):
    nx, ny, width = right.shape[1:]
    groups = width // HOP
    tall = ny // UNIT
    field = (field_0, field_1)
    chunks = chunks_of(nx)
    spans = spans_of(chunks, tall, groups)
    e = lax.axis_index("energy")
    s = lax.axis_index("space")
    me = e * n_space + s

    def greet(semaphore, step):
        @pl.when(s >= step)
        def _():
            pl.semaphore_signal(
                semaphore, inc=1, device_id=(e, s - step), device_id_type=MESH
            )

        @pl.when(s + step < n_space)
        def _():
            pl.semaphore_signal(
                semaphore, inc=1, device_id=(e, s + step), device_id_type=MESH
            )

    def greeted(step):
        return (s >= step).astype(jnp.int32) + (s + step < n_space).astype(jnp.int32)

    steps = steps_of(n_space)

    def hear(i):
        pl.semaphore_wait(known.at[i], greeted(steps[i]))
        if i + 1 < len(steps):
            greet(known.at[i + 1], steps[i + 1])

    barrier = pltpu.get_barrier_semaphore()
    def plane_at(i):
        turned, step = lax.rem(i, 2), lax.div(i, 2)
        return step + turned * (nx - 1 - 2 * step)

    def plane_of(i):
        return i // 2 if i % 2 == 0 else nx - 1 - i // 2

    copies = [
        *(
            (right_hbm.at[0:MAIN, plane_of(i)], right.at[0:MAIN, plane_of(i)])
            for i in range(nx)
        ),
        *((rate_hbm.at[plane_of(i)], rate.at[plane_of(i)]) for i in range(nx)),
        (fields_hbm, fields_ref),
        (contacts_hbm, contacts_ref),
        (offsets_hbm, offsets_ref),
        (phonon_hbm, phonon_ref),
        (regions_hbm, regions_ref),
        (speed_hbm, speed_ref),
        (right_hbm.at[MAIN], right.at[MAIN]),
    ]
    loads = [
        pltpu.make_async_copy(source, target, in_sem.at[i])
        for i, (source, target) in enumerate(copies)
    ]
    cells, small = loads[2 * nx : 2 * nx + 2], loads[2 * nx + 2 :]
    planes = [(loads[nx + i], loads[i]) for i in range(nx)]
    for load in (*cells, *(load for pair in planes for load in pair), *small):
        load.start()

    for step in range(1, n_energy):
        pl.semaphore_signal(
            barrier,
            inc=1,
            device_id=(lax.rem(e + step, n_energy), s),
            device_id_type=MESH,
        )
    greet(barrier, 1)

    zero_rows = jnp.zeros((PAD, width), jnp.float32)
    zero_plane = jnp.zeros((ny, width), jnp.float32)
    for k in range(SWEEPS):
        for c in range(COEFS):
            for x in range(1, nx + 1):
                field[k][c, x, 0:PAD] = zero_rows
                field[k][c, x, PAD + ny : 2 * PAD + ny] = zero_rows
            field[k][c, 0, PAD : PAD + ny] = zero_plane
            field[k][c, nx + 1, PAD : PAD + ny] = zero_plane

    @pl.when(e == 0)
    def _():
        for k in range(SWEEPS):
            from_low[k] = jnp.zeros(from_low.shape[1:], jnp.float32)

    @pl.when(e == n_energy - 1)
    def _():
        for k in range(SWEEPS):
            from_high[k] = jnp.zeros(from_high.shape[1:], jnp.float32)

    def spread(*pairs):
        for source, target in pairs:
            turned = source.T
            for x in range(nx):
                target[x] = jnp.broadcast_to(turned[:, x : x + 1], (ny, width))

    for load in cells:
        load.wait()
    spread((fields_ref[0], cell_x), (fields_ref[1], cell_y), (contacts_ref[...], cell_pin))

    def solve(r, px, py, diag, inv_d, inv_t):
        first = (diag * r[0] - px * r[1] - py * r[2]) * inv_t
        return first, (r[1] + px * first) * inv_d, (r[2] + py * first) * inv_d

    lane = lax.broadcasted_iota(jnp.int32, (ROWS, width), 1)
    unit_lane = lax.broadcasted_iota(jnp.int32, (UNIT, width), 1)

    def slot(at):
        at = at % width
        return (unit_lane >= at) & (unit_lane < at + HOP)

    slot_low = [slot(HOP * j) for j in range(groups)]
    slot_high = [slot(HOP * (j - 1)) for j in range(groups)]
    zero = jnp.zeros((UNIT, width), jnp.float32)

    def turn(value, by):
        by = by % width
        return pltpu.roll(value, by, 1) if by else value

    def units_of(g):
        first, last = chunks[g]
        units = [(plane_of(i), y) for i in range(first, last) for y in range(0, ny, UNIT)]
        start = spans[g][0]
        return [(start + u // groups, u % groups, *unit) for u, unit in enumerate(units)]

    def rotated(f, off):
        low, high = lane < off, lane >= width - off
        below = jnp.take_along_axis(
            f,
            jnp.where(low, lane - off + width, lane - off),
            axis=1,
            mode="promise_in_bounds",
        )
        above = jnp.take_along_axis(
            f,
            jnp.where(high, lane + off - width, lane + off),
            axis=1,
            mode="promise_in_bounds",
        )
        return jnp.where(low, 0.0, below), jnp.where(high, 0.0, above)

    def pack(k, g):
        low, high = zero, zero
        units = units_of(g)
        for u, (q, j, x, y) in enumerate(units):
            turned = turn(field[k][0, x + 1, pl.ds(PAD + y, UNIT)], HOP * j)
            low = jnp.where(slot_low[j], turned, low)
            high = jnp.where(slot_high[j], turned, high)
            if j == groups - 1 or u == len(units) - 1:
                pack_low[k, q] = low
                pack_high[k, q] = high
                low, high = zero, zero

    def prepare(g):
        place = unit_lane
        for j in range(1, groups):
            place = jnp.where(unit_lane >= HOP * j, unit_lane - HOP * j, place)
        place_low = place
        place_high = jnp.where(unit_lane >= width - HOP, unit_lane - (width - HOP), place)
        none = jnp.zeros((UNIT, width), jnp.int32)
        off_low, off_high, absorbed, emitted = none, none, zero, zero
        units = units_of(g)
        for u, (q, j, x, y) in enumerate(units):
            rows = pl.ds(y, UNIT)
            off = cell_off[x, rows]
            off_low = jnp.where(slot_low[j], off, off_low)
            off_high = jnp.where(slot_high[j], off, off_high)
            absorbed = jnp.where(slot_low[j], cell_absorb[x, rows], absorbed)
            emitted = jnp.where(slot_high[j], cell_emit[x, rows], emitted)
            if j == groups - 1 or u == len(units) - 1:
                from_low_at = unit_lane - off_low
                from_high_at = unit_lane + off_high
                turn_low[q] = jnp.where(from_low_at < 0, from_low_at + width, from_low_at)
                turn_high[q] = jnp.where(
                    from_high_at >= width, from_high_at - width, from_high_at
                )
                gain_low[q] = jnp.where(place_low < off_low, absorbed, 0.0)
                gain_high[q] = jnp.where(place_high >= HOP - off_high, emitted, 0.0)
                off_low, off_high, absorbed, emitted = none, none, zero, zero

    def first_plane(i, carry):
        x = plane_at(i)
        for y in range(0, ny, ROWS):
            rows = pl.ds(y, ROWS)
            diag = rate[x, rows] + 4.0 * diffusion
            px, py = cell_x[x, rows], cell_y[x, rows]
            inv_d = 1.0 / diag
            inv_t = 1.0 / (diag * diag + px * px + py * py)
            inv_diag[x, rows] = inv_d
            inv_det[x, rows] = inv_t
            r = [right[c, x, rows] for c in range(MAIN)]
            u = solve(r, px, py, diag, inv_d, inv_t)
            pinned = cell_pin[x, rows] == 1
            for c in range(MAIN):
                field[0][c, x + 1, pl.ds(PAD + y, ROWS)] = jnp.where(pinned, r[c], u[c])
        return carry

    def first_last(x, carry):
        for y in range(0, ny, ROWS):
            rows = pl.ds(y, ROWS)
            r = right[MAIN, x, rows]
            field[0][MAIN, x + 1, pl.ds(PAD + y, ROWS)] = jnp.where(
                cell_pin[x, rows] == 1, r, r * inv_diag[x, rows]
            )
        return carry

    inner = pl.ds(PAD, ny)
    parts = (pl.ds(0, MAIN), pl.ds(MAIN, COEFS - MAIN))

    def to_right(k, p):
        some = parts[p]
        return pltpu.make_async_remote_copy(
            src_ref=field[k].at[some, nx, inner],
            dst_ref=halo.at[k, 0, some],
            send_sem=x_send.at[k, 0, p],
            recv_sem=x_recv.at[k, 0, p],
            device_id=(e, s + 1),
            device_id_type=MESH,
        )

    def to_left(k, p):
        some = parts[p]
        return pltpu.make_async_remote_copy(
            src_ref=field[k].at[some, 1, inner],
            dst_ref=halo.at[k, 1, some],
            send_sem=x_send.at[k, 1, p],
            recv_sem=x_recv.at[k, 1, p],
            device_id=(e, s - 1),
            device_id_type=MESH,
        )

    def to_upper(k, g):
        span = pl.ds(*spans[g])
        return pltpu.make_async_remote_copy(
            src_ref=pack_high.at[k, span],
            dst_ref=from_low.at[k, span],
            send_sem=e_send.at[k, g, 0],
            recv_sem=e_recv.at[k, g, 0],
            device_id=(e + 1, s),
            device_id_type=MESH,
        )

    def to_lower(k, g):
        span = pl.ds(*spans[g])
        return pltpu.make_async_remote_copy(
            src_ref=pack_low.at[k, span],
            dst_ref=from_high.at[k, span],
            send_sem=e_send.at[k, g, 1],
            recv_sem=e_recv.at[k, g, 1],
            device_id=(e - 1, s),
            device_id_type=MESH,
        )

    has_right, has_left = s < n_space - 1, s > 0
    has_upper, has_lower = e < n_energy - 1, e > 0

    def leave_sides(k, p):
        @pl.when(has_right)
        def _():
            to_right(k, p).start()

        @pl.when(has_left)
        def _():
            to_left(k, p).start()

    odd = lax.rem(e, 2) == 1

    def leave(k, g):
        @pl.when(has_upper & odd)
        def _():
            to_upper(k, g).start()

        @pl.when(has_lower & jnp.logical_not(odd))
        def _():
            to_lower(k, g).start()

        def near(i):
            @pl.when(has_upper & jnp.logical_not(odd))
            def _():
                to_upper(k, i).start()

            @pl.when(has_lower & odd)
            def _():
                to_lower(k, i).start()

        near(g)

    def arrive(k, g):
        @pl.when(has_lower)
        def _():
            to_upper(k, g).wait_recv()

        @pl.when(has_upper)
        def _():
            to_lower(k, g).wait_recv()

    edge = min(2, nx)
    for g, (first, last) in enumerate(chunks):
        for pair in planes[first:last]:
            for load in pair:
                load.wait()
        if g == 0:
            lax.fori_loop(first, edge, first_plane, 0)
            pl.semaphore_wait(barrier, n_energy - 1 + greeted(1))
            leave_sides(0, 0)
            first = edge
        lax.fori_loop(first, last, first_plane, 0)
        pack(0, g)
        leave(0, g)
    greet(known.at[0], steps[0])
    for load in small:
        load.wait()
    lax.fori_loop(0, nx, first_last, 0)
    leave_sides(0, 1)
    region = regions_ref[...]
    free = contacts_ref[...] != 1
    off = jnp.zeros_like(region)
    absorb = jnp.zeros(region.shape, jnp.float32)
    emit = jnp.zeros(region.shape, jnp.float32)
    for r in range(REGIONS):
        inside = region == r
        off = jnp.where(inside, offsets_ref[r], off)
        absorb = jnp.where(inside & free, phonon_ref[0, r], absorb)
        emit = jnp.where(inside & free, phonon_ref[1, r], emit)
    spread((off, cell_off), (absorb, cell_absorb), (emit, cell_emit))
    for g in range(len(chunks)):
        prepare(g)
    velocity = jnp.broadcast_to(0.5 * speed_ref[...], (ROWS, width))

    def inside_part(k):
        def plane(x, carry):
            for y in range(0, ny, ROWS):
                rows = pl.ds(y, ROWS)
                mid = pl.ds(PAD + y, ROWS)
                f = [field[k][c, x + 1, mid] for c in range(COEFS)]
                xp = [field[k][c, x + 2, mid] for c in range(COEFS)]
                xm = [field[k][c, x, mid] for c in range(COEFS)]
                yp = [field[k][c, x + 1, pl.ds(PAD + y + 1, ROWS)] for c in range(COEFS)]
                ym = [field[k][c, x + 1, pl.ds(PAD + y - 1, ROWS)] for c in range(COEFS)]
                diag = rate[x, rows] + 4.0 * diffusion
                px, py = cell_x[x, rows], cell_y[x, rows]
                nb = [xp[c] + xm[c] + (yp[c] + ym[c]) for c in range(COEFS)]
                below, above = rotated(f[0], cell_off[x, rows])
                image = [
                    diag * f[0]
                    + px * f[1]
                    + py * f[2]
                    - diffusion * nb[0]
                    + velocity * (xp[1] - xm[1] + (yp[2] - ym[2]))
                    - (cell_absorb[x, rows] * below + cell_emit[x, rows] * above),
                    diag * f[1] - px * f[0] - diffusion * nb[1] + velocity * (xp[0] - xm[0]),
                    diag * f[2] - py * f[0] - diffusion * nb[2] + velocity * (yp[0] - ym[0]),
                    diag * f[3] - diffusion * nb[3],
                ]
                pinned = cell_pin[x, rows] == 1
                for c in range(COEFS):
                    part[c, x, rows] = right[c, x, rows] - jnp.where(pinned, f[c], image[c])
            return carry

        lax.fori_loop(0, nx, plane, 0)

    def beside_part(k, p):
        def side(where, x, sign):
            for y in range(0, ny, ROWS):
                rows = pl.ds(y, ROWS)
                free = cell_pin[x, rows] != 1
                if p:
                    gain = {MAIN: diffusion * halo[k, where, MAIN, rows]}
                else:
                    h = [halo[k, where, c, rows] for c in range(MAIN)]
                    swing = sign * velocity
                    gain = {
                        0: diffusion * h[0] - swing * h[1],
                        1: diffusion * h[1] - swing * h[0],
                        2: diffusion * h[2],
                    }
                for c, value in gain.items():
                    part[c, x, rows] = part[c, x, rows] + jnp.where(free, value, 0.0)

        @pl.when(has_left)
        def _():
            to_right(k, p).wait_recv()
            side(0, 0, -1.0)

        @pl.when(has_right)
        def _():
            to_left(k, p).wait_recv()
            side(1, nx - 1, 1.0)

    def outside_last(k):
        def plane(x, acc):
            for y in range(0, ny, UNIT):
                rows, mid = pl.ds(y, UNIT), pl.ds(PAD + y, UNIT)
                r = part[MAIN, x, rows]
                acc = acc + r * r
                if k < SWEEPS - 1:
                    field[k + 1][MAIN, x + 1, mid] = field[k][MAIN, x + 1, mid] + jnp.where(
                        cell_pin[x, rows] == 1, r, r * inv_diag[x, rows]
                    )
            return acc

        return lax.fori_loop(0, nx, plane, zero)

    def outside_part(k, g, acc):
        def take(source, at, gain):
            return gain * jnp.take_along_axis(
                source, at, axis=1, mode="promise_in_bounds"
            )

        start, count = spans[g]
        here = range(start, start + count)
        low = [take(from_low[k, q], turn_low[q], gain_low[q]) for q in here]
        high = [take(from_high[k, q], turn_high[q], gain_high[q]) for q in here]
        acc = list(acc)
        for i, (q, j, x, y) in enumerate(units_of(g)):
            rows, mid = pl.ds(y, UNIT), pl.ds(PAD + y, UNIT)
            came = jnp.where(
                slot_low[j], low[q - start], jnp.where(slot_high[j], high[q - start], 0.0)
            )
            r = [part[c, x, rows] for c in range(MAIN)]
            r[0] = r[0] + turn(came, -HOP * j)
            for c in range(MAIN):
                acc[c] = acc[c] + r[c] * r[c]
            if k < SWEEPS - 1:
                diag = rate[x, rows] + 4.0 * diffusion
                px, py = cell_x[x, rows], cell_y[x, rows]
                u = solve(r, px, py, diag, inv_diag[x, rows], inv_det[x, rows])
                pinned = cell_pin[x, rows] == 1
                for c in range(MAIN):
                    field[k + 1][c, x + 1, mid] = field[k][c, x + 1, mid] + jnp.where(
                        pinned, r[c], u[c]
                    )
                if g == 0 and i == edge * tall - 1:
                    leave_sides(k + 1, 0)
        return tuple(acc)

    spot = lax.broadcasted_iota(jnp.int32, (SWEEPS * COEFS, width), 0)
    mine = jnp.zeros((SWEEPS * COEFS, width), jnp.float32)
    store = pltpu.make_async_copy(
        field[SWEEPS - 1].at[:, pl.ds(1, nx), inner], state_ref, out_sem
    )
    for k in range(SWEEPS):
        if k == SWEEPS - 1:
            store.start()
        inside_part(k)
        if 0 < k < len(steps):
            hear(k)
        beside_part(k, 0)
        if k == 0:
            hear(0)
        acc = (zero,) * MAIN
        for g in range(len(chunks)):
            if k == SWEEPS - 1 and g == len(chunks) - 1:
                beside_part(k, 1)
                tail = outside_last(k)
            arrive(k, g)
            acc = outside_part(k, g, acc)
            if k < SWEEPS - 1:
                pack(k + 1, g)
                leave(k + 1, g)
        if k < SWEEPS - 1:
            beside_part(k, 1)
            tail = outside_last(k)
            leave_sides(k + 1, 1)
        for c, value in enumerate((*acc, tail)):
            mine = jnp.where(
                spot == COEFS * k + c, jnp.sum(value, axis=0, keepdims=True), mine
            )

    lines = SWEEPS * COEFS
    share = width // lines
    by = width // 2
    while by >= share:
        mine = mine + pltpu.roll(mine, by, 1)
        by //= 2
    at = lax.broadcasted_iota(jnp.int32, (lines, width), 1)
    own_lanes = (at >= spot * share) & (at < (spot + 1) * share)
    sums[me] = jnp.sum(jnp.where(own_lanes, mine, 0.0), axis=0, keepdims=True)
    for i in range(SWEEPS, len(steps)):
        hear(i)

    def tell(to_e, to_s, rows):
        return pltpu.make_async_remote_copy(
            src_ref=sums.at[rows],
            dst_ref=sums.at[rows],
            send_sem=n_send,
            recv_sem=n_recv,
            device_id=(to_e, to_s),
            device_id_type=MESH,
        )

    def others_of(at, size):
        return [jnp.where(i < at, i, i + 1) for i in range(size - 1)]

    own = pl.ds(me, 1)
    for to_e in others_of(e, n_energy):
        tell(to_e, s, own).start()
    for to_s in others_of(s, n_space):
        for to_e in range(n_energy):
            tell(to_e, to_s, own).start()
    for k in range(SWEEPS):

        for p in range(len(parts)):

            @pl.when(has_right)
            def _():
                to_right(k, p).wait_send()

            @pl.when(has_left)
            def _():
                to_left(k, p).wait_send()

        for g in range(len(chunks)):

            @pl.when(has_upper)
            def _():
                to_upper(k, g).wait_send()

            @pl.when(has_lower)
            def _():
                to_lower(k, g).wait_send()

    store.wait()
    others = tell(e, lax.rem(s + 1, n_space), pl.ds(0, n_energy * n_space - 1))
    others.wait_recv()
    others.wait_send()
    sums_ref[...] = jnp.sum(sums[...], axis=0)


def finish(state, sums_ref, state_hbm, norms_hbm, norms, sem):
    stores = [
        pltpu.make_async_copy(state.at[c], state_hbm.at[c], sem.at[c]) for c in range(COEFS)
    ]
    for store in stores:
        store.start()
    width = sums_ref.shape[1]
    lines = SWEEPS * COEFS
    share = width // lines
    shape = (lines, width)
    row = lax.broadcasted_iota(jnp.int32, shape, 0)
    lane = lax.broadcasted_iota(jnp.int32, shape, 1)
    own_lanes = (lane >= row * share) & (lane < (row + 1) * share)
    spread = jnp.where(own_lanes, jnp.broadcast_to(sums_ref[...], shape), 0.0)
    norm = jnp.broadcast_to(jnp.sqrt(jnp.sum(spread, axis=1, keepdims=True)), shape)
    for k in range(SWEEPS):
        line = jnp.sum(
            jnp.where(row == lane + COEFS * k, norm, 0.0), axis=0, keepdims=True
        )
        norms[k : k + 1, :] = line[:, 0:COEFS]
    store = pltpu.make_async_copy(norms, norms_hbm, sem.at[COEFS])
    store.start()
    for load in (*stores, store):
        load.wait()


def steps_of(n_space):
    steps = [1]
    while 2 * steps[-1] < n_space:
        steps.append(2 * steps[-1])
    return steps


def chunks_of(nx):
    edge = min(2, nx)
    cuts = [0, edge, edge + (nx - edge) // 2, nx]
    return [(a, b) for a, b in zip(cuts[:-1], cuts[1:]) if b > a]


def spans_of(chunks, tall, groups):
    out, start = [], 0
    for first, last in chunks:
        count = -(-(last - first) * tall // groups)
        out.append((start, count))
        start += count
    return out


def solution(mesh):
    n_energy, n_space = mesh.shape["energy"], mesh.shape["space"]

    def local(right_side, rate, fields, speed, regions, contacts, offsets, phonon):
        coefs, nx, ny, width = right_side.shape
        spans = spans_of(chunks_of(nx), ny // UNIT, width // HOP)
        chunks, packs = len(spans), sum(spans[-1])
        plane = (nx, ny, width)
        vmem = pl.BlockSpec(memory_space=pltpu.VMEM)
        hbm = pl.BlockSpec(memory_space=pl.ANY)
        f32 = jnp.float32
        pack = pltpu.VMEM((SWEEPS, packs, UNIT, width), f32)
        state, sums = pl.pallas_call(
            functools.partial(kernel, n_energy, n_space),
            out_shape=(
                pltpu.VMEM(right_side.shape, f32),
                pltpu.VMEM((1, width), f32),
            ),
            in_specs=[pl.BlockSpec(memory_space=pltpu.HBM)] * 8,
            out_specs=(vmem, vmem),
            scratch_shapes=[
                pltpu.SMEM(offsets.shape, offsets.dtype),
                pltpu.SMEM((phonon.shape[1], phonon.shape[0]), f32),
                pltpu.VMEM(fields.shape, f32),
                pltpu.VMEM((1, width), f32),
                pltpu.VMEM(regions.shape, regions.dtype),
                pltpu.VMEM(contacts.shape, contacts.dtype),
                pltpu.VMEM(right_side.shape, f32),
                pltpu.VMEM(plane, f32),
                pltpu.VMEM((coefs, nx + 2, ny + 2 * PAD, width), f32),
                pltpu.VMEM((coefs, nx + 2, ny + 2 * PAD, width), f32),
                pltpu.VMEM(right_side.shape, f32),
                pltpu.VMEM((SWEEPS, 2, coefs, ny, width), f32),
                pltpu.VMEM(plane, f32),
                pltpu.VMEM(plane, f32),
                pltpu.VMEM(plane, jnp.int32),
                pltpu.VMEM(plane, jnp.int32),
                pltpu.VMEM(plane, f32),
                pltpu.VMEM(plane, f32),
                pltpu.VMEM(plane, f32),
                pltpu.VMEM(plane, f32),
                pltpu.VMEM((packs, UNIT, width), jnp.int32),
                pltpu.VMEM((packs, UNIT, width), jnp.int32),
                pltpu.VMEM((packs, UNIT, width), f32),
                pltpu.VMEM((packs, UNIT, width), f32),
                pack,
                pack,
                pack,
                pack,
                pltpu.VMEM((n_energy * n_space, 1, width), f32),
                pltpu.SemaphoreType.DMA((7 + 2 * nx,)),
                pltpu.SemaphoreType.DMA,
                pltpu.SemaphoreType.DMA((SWEEPS, 2, 2)),
                pltpu.SemaphoreType.DMA((SWEEPS, 2, 2)),
                pltpu.SemaphoreType.DMA((SWEEPS, chunks, 2)),
                pltpu.SemaphoreType.DMA((SWEEPS, chunks, 2)),
                pltpu.SemaphoreType.DMA,
                pltpu.SemaphoreType.DMA,
                pltpu.SemaphoreType.REGULAR((len(steps_of(n_space)),)),
            ],
            compiler_params=pltpu.CompilerParams(
                collective_id=0, has_side_effects=True, vmem_limit_bytes=24 << 20
            ),
        )(
            *(
                pltpu.with_memory_space_constraint(value, pltpu.HBM)
                for value in (
                    offsets,
                    phonon.T,
                    right_side,
                    rate,
                    fields,
                    speed.reshape(1, width),
                    regions,
                    contacts,
                )
            )
        )
        return pl.pallas_call(
            finish,
            out_shape=(
                jax.ShapeDtypeStruct(right_side.shape, f32),
                jax.ShapeDtypeStruct((SWEEPS, coefs), f32),
            ),
            in_specs=[vmem, vmem],
            out_specs=(hbm, hbm),
            scratch_shapes=[
                pltpu.VMEM((SWEEPS, coefs), f32),
                pltpu.SemaphoreType.DMA((coefs + 1,)),
            ],
            compiler_params=pltpu.CompilerParams(vmem_limit_bytes=8 << 20),
        )(state, sums)

    in_specs = (
        P(None, "space", None, "energy"),
        P("space", None, "energy"),
        P(None, "space", None),
        P("energy"),
        P("space", None),
        P("space", None),
        P(),
        P(),
    )
    out_specs = (P(None, "space", None, "energy"), P())
    return jax.shard_map(local, mesh=mesh, in_specs=in_specs, out_specs=out_specs, check_vma=False)
```

```python
import functools

import jax
import jax.numpy as jnp
from jax import lax
from jax.experimental import pallas as pl
from jax.experimental.pallas import tpu as pltpu
from jax.sharding import PartitionSpec as P

HOP = 24
REGIONS = 4
SWEEPS = 2
COEFS = 4
MAIN = 3
PAD = 8
ROWS = 16
UNIT = 8

diffusion = 0.25

MESH = pl.DeviceIdType.MESH


def kernel(
    n_energy,
    n_space,
    offsets_hbm,
    phonon_hbm,
    right_hbm,
    rate_hbm,
    fields_hbm,
    speed_hbm,
    regions_hbm,
    contacts_hbm,
    state_ref,
    sums_ref,
    offsets_ref,
    phonon_ref,
    fields_ref,
    speed_ref,
    regions_ref,
    contacts_ref,
    right,
    rate,
    field_0,
    field_1,
    part,
    halo,
    cell_x,
    cell_y,
    cell_pin,
    cell_off,
    cell_absorb,
    cell_emit,
    inv_diag,
    inv_det,
    turn_low,
    turn_high,
    gain_low,
    gain_high,
    pack_low,
    pack_high,
    from_low,
    from_high,
    sums,
    in_sem,
    out_sem,
    x_send,
    x_recv,
    e_send,
    e_recv,
    n_send,
    n_recv,
    known,
):
    nx, ny, width = right.shape[1:]
    groups = width // HOP
    tall = ny // UNIT
    field = (field_0, field_1)
    chunks = chunks_of(nx)
    spans = spans_of(chunks, tall, groups)
    e = lax.axis_index("energy")
    s = lax.axis_index("space")
    me = e * n_space + s

    def greet(semaphore, along, step):
        at, size = (e, n_energy) if along else (s, n_space)

        @pl.when(at >= step)
        def _():
            to = (e - step, s) if along else (e, s - step)
            pl.semaphore_signal(semaphore, inc=1, device_id=to, device_id_type=MESH)

        @pl.when(at + step < size)
        def _():
            to = (e + step, s) if along else (e, s + step)
            pl.semaphore_signal(semaphore, inc=1, device_id=to, device_id_type=MESH)

    def greeted(along, step):
        at, size = (e, n_energy) if along else (s, n_space)
        return (at >= step).astype(jnp.int32) + (at + step < size).astype(jnp.int32)

    steps = steps_of(n_energy, n_space)

    def hear(i):
        if i < len(steps):
            pl.semaphore_wait(known.at[i], greeted(*steps[i]))
        if i + 1 < len(steps):
            greet(known.at[i + 1], *steps[i + 1])

    barrier = pltpu.get_barrier_semaphore()
    def plane_at(i):
        turned, step = lax.rem(i, 2), lax.div(i, 2)
        return step + turned * (nx - 1 - 2 * step)

    def plane_of(i):
        return i // 2 if i % 2 == 0 else nx - 1 - i // 2

    copies = [
        *(
            (right_hbm.at[0:MAIN, plane_of(i)], right.at[0:MAIN, plane_of(i)])
            for i in range(nx)
        ),
        *((rate_hbm.at[plane_of(i)], rate.at[plane_of(i)]) for i in range(nx)),
        (fields_hbm, fields_ref),
        (contacts_hbm, contacts_ref),
        (offsets_hbm, offsets_ref),
        (phonon_hbm, phonon_ref),
        (regions_hbm, regions_ref),
        (speed_hbm, speed_ref),
        (right_hbm.at[MAIN], right.at[MAIN]),
    ]
    loads = [
        pltpu.make_async_copy(source, target, in_sem.at[i])
        for i, (source, target) in enumerate(copies)
    ]
    cells, small = loads[2 * nx : 2 * nx + 2], loads[2 * nx + 2 :]
    planes = [(loads[nx + i], loads[i]) for i in range(nx)]
    greet(barrier, 1, 1)
    greet(barrier, 0, 1)
    for load in (*cells, *(load for pair in planes for load in pair), *small):
        load.start()


    zero_rows = jnp.zeros((PAD, width), jnp.float32)
    zero_plane = jnp.zeros((ny, width), jnp.float32)
    for k in range(SWEEPS):
        for c in range(COEFS):
            for x in range(1, nx + 1):
                field[k][c, x, 0:PAD] = zero_rows
                field[k][c, x, PAD + ny : 2 * PAD + ny] = zero_rows
            field[k][c, 0, PAD : PAD + ny] = zero_plane
            field[k][c, nx + 1, PAD : PAD + ny] = zero_plane

    @pl.when(e == 0)
    def _():
        for k in range(SWEEPS):
            from_low[k] = jnp.zeros(from_low.shape[1:], jnp.float32)

    @pl.when(e == n_energy - 1)
    def _():
        for k in range(SWEEPS):
            from_high[k] = jnp.zeros(from_high.shape[1:], jnp.float32)

    def spread(*pairs):
        for source, target in pairs:
            turned = source.T
            for x in range(nx):
                target[x] = jnp.broadcast_to(turned[:, x : x + 1], (ny, width))

    for load in cells:
        load.wait()
    spread((fields_ref[0], cell_x), (fields_ref[1], cell_y), (contacts_ref[...], cell_pin))

    def solve(r, px, py, diag, inv_d, inv_t):
        first = (diag * r[0] - px * r[1] - py * r[2]) * inv_t
        return first, (r[1] + px * first) * inv_d, (r[2] + py * first) * inv_d

    lane = lax.broadcasted_iota(jnp.int32, (ROWS, width), 1)
    unit_lane = lax.broadcasted_iota(jnp.int32, (UNIT, width), 1)

    def slot(at):
        at = at % width
        return (unit_lane >= at) & (unit_lane < at + HOP)

    slot_low = [slot(HOP * j) for j in range(groups)]
    slot_high = [slot(HOP * (j - 1)) for j in range(groups)]
    zero = jnp.zeros((UNIT, width), jnp.float32)

    def turn(value, by):
        by = by % width
        return pltpu.roll(value, by, 1) if by else value

    def units_of(g):
        first, last = chunks[g]
        units = [(plane_of(i), y) for i in range(first, last) for y in range(0, ny, UNIT)]
        start = spans[g][0]
        return [(start + u // groups, u % groups, *unit) for u, unit in enumerate(units)]

    def rotated(f, off):
        low, high = lane < off, lane >= width - off
        below = jnp.take_along_axis(
            f,
            jnp.where(low, lane - off + width, lane - off),
            axis=1,
            mode="promise_in_bounds",
        )
        above = jnp.take_along_axis(
            f,
            jnp.where(high, lane + off - width, lane + off),
            axis=1,
            mode="promise_in_bounds",
        )
        return jnp.where(low, 0.0, below), jnp.where(high, 0.0, above)

    def pack(k, g):
        low, high = zero, zero
        units = units_of(g)
        for u, (q, j, x, y) in enumerate(units):
            turned = turn(field[k][0, x + 1, pl.ds(PAD + y, UNIT)], HOP * j)
            low = jnp.where(slot_low[j], turned, low)
            high = jnp.where(slot_high[j], turned, high)
            if j == groups - 1 or u == len(units) - 1:
                pack_low[k, q] = low
                pack_high[k, q] = high
                low, high = zero, zero

    def prepare(g):
        place = unit_lane
        for j in range(1, groups):
            place = jnp.where(unit_lane >= HOP * j, unit_lane - HOP * j, place)
        place_low = place
        place_high = jnp.where(unit_lane >= width - HOP, unit_lane - (width - HOP), place)
        none = jnp.zeros((UNIT, width), jnp.int32)
        off_low, off_high, absorbed, emitted = none, none, zero, zero
        units = units_of(g)
        for u, (q, j, x, y) in enumerate(units):
            rows = pl.ds(y, UNIT)
            off = cell_off[x, rows]
            off_low = jnp.where(slot_low[j], off, off_low)
            off_high = jnp.where(slot_high[j], off, off_high)
            absorbed = jnp.where(slot_low[j], cell_absorb[x, rows], absorbed)
            emitted = jnp.where(slot_high[j], cell_emit[x, rows], emitted)
            if j == groups - 1 or u == len(units) - 1:
                from_low_at = unit_lane - off_low
                from_high_at = unit_lane + off_high
                turn_low[q] = jnp.where(from_low_at < 0, from_low_at + width, from_low_at)
                turn_high[q] = jnp.where(
                    from_high_at >= width, from_high_at - width, from_high_at
                )
                gain_low[q] = jnp.where(place_low < off_low, absorbed, 0.0)
                gain_high[q] = jnp.where(place_high >= HOP - off_high, emitted, 0.0)
                off_low, off_high, absorbed, emitted = none, none, zero, zero

    def first_plane(i, carry):
        x = plane_at(i)
        for y in range(0, ny, ROWS):
            rows = pl.ds(y, ROWS)
            diag = rate[x, rows] + 4.0 * diffusion
            px, py = cell_x[x, rows], cell_y[x, rows]
            inv_d = 1.0 / diag
            inv_t = 1.0 / (diag * diag + px * px + py * py)
            inv_diag[x, rows] = inv_d
            inv_det[x, rows] = inv_t
            r = [right[c, x, rows] for c in range(MAIN)]
            u = solve(r, px, py, diag, inv_d, inv_t)
            pinned = cell_pin[x, rows] == 1
            for c in range(MAIN):
                field[0][c, x + 1, pl.ds(PAD + y, ROWS)] = jnp.where(pinned, r[c], u[c])
        return carry

    def first_last(x, carry):
        for y in range(0, ny, ROWS):
            rows = pl.ds(y, ROWS)
            r = right[MAIN, x, rows]
            field[0][MAIN, x + 1, pl.ds(PAD + y, ROWS)] = jnp.where(
                cell_pin[x, rows] == 1, r, r * inv_diag[x, rows]
            )
        return carry

    inner = pl.ds(PAD, ny)
    parts = (pl.ds(0, MAIN), pl.ds(MAIN, COEFS - MAIN))

    def to_right(k, p):
        some = parts[p]
        return pltpu.make_async_remote_copy(
            src_ref=field[k].at[some, nx, inner],
            dst_ref=halo.at[k, 0, some],
            send_sem=x_send.at[k, 0, p],
            recv_sem=x_recv.at[k, 0, p],
            device_id=(e, s + 1),
            device_id_type=MESH,
        )

    def to_left(k, p):
        some = parts[p]
        return pltpu.make_async_remote_copy(
            src_ref=field[k].at[some, 1, inner],
            dst_ref=halo.at[k, 1, some],
            send_sem=x_send.at[k, 1, p],
            recv_sem=x_recv.at[k, 1, p],
            device_id=(e, s - 1),
            device_id_type=MESH,
        )

    def to_upper(k, g):
        span = pl.ds(*spans[g])
        return pltpu.make_async_remote_copy(
            src_ref=pack_high.at[k, span],
            dst_ref=from_low.at[k, span],
            send_sem=e_send.at[k, g, 0],
            recv_sem=e_recv.at[k, g, 0],
            device_id=(e + 1, s),
            device_id_type=MESH,
        )

    def to_lower(k, g):
        span = pl.ds(*spans[g])
        return pltpu.make_async_remote_copy(
            src_ref=pack_low.at[k, span],
            dst_ref=from_high.at[k, span],
            send_sem=e_send.at[k, g, 1],
            recv_sem=e_recv.at[k, g, 1],
            device_id=(e - 1, s),
            device_id_type=MESH,
        )

    has_right, has_left = s < n_space - 1, s > 0
    has_upper, has_lower = e < n_energy - 1, e > 0

    def leave_sides(k, p):
        @pl.when(has_right)
        def _():
            to_right(k, p).start()

        @pl.when(has_left)
        def _():
            to_left(k, p).start()

    odd = lax.rem(e, 2) == 1

    def leave(k, g):
        @pl.when(has_upper & odd)
        def _():
            to_upper(k, g).start()

        @pl.when(has_lower & jnp.logical_not(odd))
        def _():
            to_lower(k, g).start()

        def near(i):
            @pl.when(has_upper & jnp.logical_not(odd))
            def _():
                to_upper(k, i).start()

            @pl.when(has_lower & odd)
            def _():
                to_lower(k, i).start()

        near(g)

    def arrive(k, g):
        @pl.when(has_lower)
        def _():
            to_upper(k, g).wait_recv()

        @pl.when(has_upper)
        def _():
            to_lower(k, g).wait_recv()

    edge = min(2, nx)
    for g, (first, last) in enumerate(chunks):
        for pair in planes[first:last]:
            for load in pair:
                load.wait()
        if g == 0:
            lax.fori_loop(first, edge, first_plane, 0)
            pl.semaphore_wait(barrier, greeted(1, 1) + greeted(0, 1))
            leave_sides(0, 0)
            first = edge
        lax.fori_loop(first, last, first_plane, 0)
        pack(0, g)
        leave(0, g)
    greet(known.at[0], *steps[0])
    for load in small:
        load.wait()
    lax.fori_loop(0, nx, first_last, 0)
    leave_sides(0, 1)
    region = regions_ref[...]
    free = contacts_ref[...] != 1
    off = jnp.zeros_like(region)
    absorb = jnp.zeros(region.shape, jnp.float32)
    emit = jnp.zeros(region.shape, jnp.float32)
    for r in range(REGIONS):
        inside = region == r
        off = jnp.where(inside, offsets_ref[r], off)
        absorb = jnp.where(inside & free, phonon_ref[0, r], absorb)
        emit = jnp.where(inside & free, phonon_ref[1, r], emit)
    spread((off, cell_off), (absorb, cell_absorb), (emit, cell_emit))
    for g in range(len(chunks)):
        prepare(g)
    velocity = jnp.broadcast_to(0.5 * speed_ref[...], (ROWS, width))

    def inside_part(k):
        def plane(x, carry):
            for y in range(0, ny, ROWS):
                rows = pl.ds(y, ROWS)
                mid = pl.ds(PAD + y, ROWS)
                f = [field[k][c, x + 1, mid] for c in range(COEFS)]
                xp = [field[k][c, x + 2, mid] for c in range(COEFS)]
                xm = [field[k][c, x, mid] for c in range(COEFS)]
                yp = [field[k][c, x + 1, pl.ds(PAD + y + 1, ROWS)] for c in range(COEFS)]
                ym = [field[k][c, x + 1, pl.ds(PAD + y - 1, ROWS)] for c in range(COEFS)]
                diag = rate[x, rows] + 4.0 * diffusion
                px, py = cell_x[x, rows], cell_y[x, rows]
                nb = [xp[c] + xm[c] + (yp[c] + ym[c]) for c in range(COEFS)]
                below, above = rotated(f[0], cell_off[x, rows])
                image = [
                    diag * f[0]
                    + px * f[1]
                    + py * f[2]
                    - diffusion * nb[0]
                    + velocity * (xp[1] - xm[1] + (yp[2] - ym[2]))
                    - (cell_absorb[x, rows] * below + cell_emit[x, rows] * above),
                    diag * f[1] - px * f[0] - diffusion * nb[1] + velocity * (xp[0] - xm[0]),
                    diag * f[2] - py * f[0] - diffusion * nb[2] + velocity * (yp[0] - ym[0]),
                    diag * f[3] - diffusion * nb[3],
                ]
                pinned = cell_pin[x, rows] == 1
                for c in range(COEFS):
                    part[c, x, rows] = right[c, x, rows] - jnp.where(pinned, f[c], image[c])
            return carry

        lax.fori_loop(0, nx, plane, 0)

    def beside_part(k, p):
        def side(where, x, sign):
            for y in range(0, ny, ROWS):
                rows = pl.ds(y, ROWS)
                free = cell_pin[x, rows] != 1
                if p:
                    gain = {MAIN: diffusion * halo[k, where, MAIN, rows]}
                else:
                    h = [halo[k, where, c, rows] for c in range(MAIN)]
                    swing = sign * velocity
                    gain = {
                        0: diffusion * h[0] - swing * h[1],
                        1: diffusion * h[1] - swing * h[0],
                        2: diffusion * h[2],
                    }
                for c, value in gain.items():
                    part[c, x, rows] = part[c, x, rows] + jnp.where(free, value, 0.0)

        @pl.when(has_left)
        def _():
            to_right(k, p).wait_recv()
            side(0, 0, -1.0)

        @pl.when(has_right)
        def _():
            to_left(k, p).wait_recv()
            side(1, nx - 1, 1.0)

    def outside_last(k):
        def plane(x, acc):
            for y in range(0, ny, UNIT):
                rows, mid = pl.ds(y, UNIT), pl.ds(PAD + y, UNIT)
                r = part[MAIN, x, rows]
                acc = acc + r * r
                if k < SWEEPS - 1:
                    field[k + 1][MAIN, x + 1, mid] = field[k][MAIN, x + 1, mid] + jnp.where(
                        cell_pin[x, rows] == 1, r, r * inv_diag[x, rows]
                    )
            return acc

        return lax.fori_loop(0, nx, plane, zero)

    def outside_part(k, g, acc):
        def take(source, at, gain):
            return gain * jnp.take_along_axis(
                source, at, axis=1, mode="promise_in_bounds"
            )

        start, count = spans[g]
        here = range(start, start + count)
        low = [take(from_low[k, q], turn_low[q], gain_low[q]) for q in here]
        high = [take(from_high[k, q], turn_high[q], gain_high[q]) for q in here]
        acc = list(acc)
        for i, (q, j, x, y) in enumerate(units_of(g)):
            rows, mid = pl.ds(y, UNIT), pl.ds(PAD + y, UNIT)
            came = jnp.where(
                slot_low[j], low[q - start], jnp.where(slot_high[j], high[q - start], 0.0)
            )
            r = [part[c, x, rows] for c in range(MAIN)]
            r[0] = r[0] + turn(came, -HOP * j)
            for c in range(MAIN):
                acc[c] = acc[c] + r[c] * r[c]
            if k < SWEEPS - 1:
                diag = rate[x, rows] + 4.0 * diffusion
                px, py = cell_x[x, rows], cell_y[x, rows]
                u = solve(r, px, py, diag, inv_diag[x, rows], inv_det[x, rows])
                pinned = cell_pin[x, rows] == 1
                for c in range(MAIN):
                    field[k + 1][c, x + 1, mid] = field[k][c, x + 1, mid] + jnp.where(
                        pinned, r[c], u[c]
                    )
                if g == 0 and i == edge * tall - 1:
                    leave_sides(k + 1, 0)
        return tuple(acc)

    share = width // (SWEEPS * COEFS)
    mine = zero

    def folded(value):
        by = width // 2
        while by >= share:
            value = value + pltpu.roll(value, by, 1)
            by //= 2
        return value

    store = pltpu.make_async_copy(
        field[SWEEPS - 1].at[:, pl.ds(1, nx), inner], state_ref, out_sem
    )
    for k in range(SWEEPS):
        if k == SWEEPS - 1:
            store.start()
        inside_part(k)
        if k == 0:
            hear(0)
        elif k == 1:
            hear(3)
        beside_part(k, 0)
        if k == 0:
            hear(1)
        acc = (zero,) * MAIN
        for g in range(len(chunks)):
            if k == SWEEPS - 1 and g == len(chunks) - 1:
                beside_part(k, 1)
                tail = outside_last(k)
            arrive(k, g)
            acc = outside_part(k, g, acc)
            if k < SWEEPS - 1:
                pack(k + 1, g)
                leave(k + 1, g)
        if k < SWEEPS - 1:
            beside_part(k, 1)
            tail = outside_last(k)
            leave_sides(k + 1, 1)
            if k == 0:
                hear(2)
        for c, value in enumerate((*acc, tail)):
            at = (COEFS * k + c) * share
            here = (unit_lane >= at) & (unit_lane < at + share)
            mine = jnp.where(here, folded(value), mine)

    sums[me] = jnp.sum(mine, axis=0, keepdims=True)
    for i in range(4, len(steps)):
        hear(i)

    def tell(to_e, to_s, rows):
        return pltpu.make_async_remote_copy(
            src_ref=sums.at[rows],
            dst_ref=sums.at[rows],
            send_sem=n_send,
            recv_sem=n_recv,
            device_id=(to_e, to_s),
            device_id_type=MESH,
        )

    def others_of(at, size):
        return [jnp.where(i < at, i, i + 1) for i in range(size - 1)]

    own = pl.ds(me, 1)
    for to_e in others_of(e, n_energy):
        tell(to_e, s, own).start()
    for to_s in others_of(s, n_space):
        for to_e in range(n_energy):
            tell(to_e, to_s, own).start()
    for k in range(SWEEPS):

        for p in range(len(parts)):

            @pl.when(has_right)
            def _():
                to_right(k, p).wait_send()

            @pl.when(has_left)
            def _():
                to_left(k, p).wait_send()

        for g in range(len(chunks)):

            @pl.when(has_upper)
            def _():
                to_upper(k, g).wait_send()

            @pl.when(has_lower)
            def _():
                to_lower(k, g).wait_send()

    store.wait()
    others = tell(e, lax.rem(s + 1, n_space), pl.ds(0, n_energy * n_space - 1))
    others.wait_recv()
    others.wait_send()
    sums_ref[...] = jnp.sum(sums[...], axis=0)


def finish(state, sums_ref, state_hbm, norms_hbm, norms, sem):
    stores = [
        pltpu.make_async_copy(state.at[c], state_hbm.at[c], sem.at[c]) for c in range(COEFS)
    ]
    for store in stores:
        store.start()
    width = sums_ref.shape[1]
    lines = SWEEPS * COEFS
    share = width // lines
    shape = (lines, width)
    row = lax.broadcasted_iota(jnp.int32, shape, 0)
    lane = lax.broadcasted_iota(jnp.int32, shape, 1)
    own_lanes = (lane >= row * share) & (lane < (row + 1) * share)
    spread = jnp.where(own_lanes, jnp.broadcast_to(sums_ref[...], shape), 0.0)
    norm = jnp.broadcast_to(jnp.sqrt(jnp.sum(spread, axis=1, keepdims=True)), shape)
    for k in range(SWEEPS):
        line = jnp.sum(
            jnp.where(row == lane + COEFS * k, norm, 0.0), axis=0, keepdims=True
        )
        norms[k : k + 1, :] = line[:, 0:COEFS]
    store = pltpu.make_async_copy(norms, norms_hbm, sem.at[COEFS])
    store.start()
    for load in (*stores, store):
        load.wait()


def steps_of(n_energy, n_space):
    out = []
    for along, size in ((1, n_energy), (0, n_space)):
        step = 1
        out.append((along, step))
        while 2 * step < size:
            step *= 2
            out.append((along, step))
    return out


def chunks_of(nx):
    edge = min(2, nx)
    cuts = [0, edge, edge + (nx - edge) // 2, nx]
    return [(a, b) for a, b in zip(cuts[:-1], cuts[1:]) if b > a]


def spans_of(chunks, tall, groups):
    out, start = [], 0
    for first, last in chunks:
        count = -(-(last - first) * tall // groups)
        out.append((start, count))
        start += count
    return out


def solution(mesh):
    n_energy, n_space = mesh.shape["energy"], mesh.shape["space"]

    def local(right_side, rate, fields, speed, regions, contacts, offsets, phonon):
        coefs, nx, ny, width = right_side.shape
        spans = spans_of(chunks_of(nx), ny // UNIT, width // HOP)
        chunks, packs = len(spans), sum(spans[-1])
        plane = (nx, ny, width)
        vmem = pl.BlockSpec(memory_space=pltpu.VMEM)
        hbm = pl.BlockSpec(memory_space=pl.ANY)
        f32 = jnp.float32
        pack = pltpu.VMEM((SWEEPS, packs, UNIT, width), f32)
        state, sums = pl.pallas_call(
            functools.partial(kernel, n_energy, n_space),
            out_shape=(
                pltpu.VMEM(right_side.shape, f32),
                pltpu.VMEM((1, width), f32),
            ),
            in_specs=[pl.BlockSpec(memory_space=pltpu.HBM)] * 8,
            out_specs=(vmem, vmem),
            scratch_shapes=[
                pltpu.SMEM(offsets.shape, offsets.dtype),
                pltpu.SMEM((phonon.shape[1], phonon.shape[0]), f32),
                pltpu.VMEM(fields.shape, f32),
                pltpu.VMEM((1, width), f32),
                pltpu.VMEM(regions.shape, regions.dtype),
                pltpu.VMEM(contacts.shape, contacts.dtype),
                pltpu.VMEM(right_side.shape, f32),
                pltpu.VMEM(plane, f32),
                pltpu.VMEM((coefs, nx + 2, ny + 2 * PAD, width), f32),
                pltpu.VMEM((coefs, nx + 2, ny + 2 * PAD, width), f32),
                pltpu.VMEM(right_side.shape, f32),
                pltpu.VMEM((SWEEPS, 2, coefs, ny, width), f32),
                pltpu.VMEM(plane, f32),
                pltpu.VMEM(plane, f32),
                pltpu.VMEM(plane, jnp.int32),
                pltpu.VMEM(plane, jnp.int32),
                pltpu.VMEM(plane, f32),
                pltpu.VMEM(plane, f32),
                pltpu.VMEM(plane, f32),
                pltpu.VMEM(plane, f32),
                pltpu.VMEM((packs, UNIT, width), jnp.int32),
                pltpu.VMEM((packs, UNIT, width), jnp.int32),
                pltpu.VMEM((packs, UNIT, width), f32),
                pltpu.VMEM((packs, UNIT, width), f32),
                pack,
                pack,
                pack,
                pack,
                pltpu.VMEM((n_energy * n_space, 1, width), f32),
                pltpu.SemaphoreType.DMA((7 + 2 * nx,)),
                pltpu.SemaphoreType.DMA,
                pltpu.SemaphoreType.DMA((SWEEPS, 2, 2)),
                pltpu.SemaphoreType.DMA((SWEEPS, 2, 2)),
                pltpu.SemaphoreType.DMA((SWEEPS, chunks, 2)),
                pltpu.SemaphoreType.DMA((SWEEPS, chunks, 2)),
                pltpu.SemaphoreType.DMA,
                pltpu.SemaphoreType.DMA,
                pltpu.SemaphoreType.REGULAR((len(steps_of(n_energy, n_space)),)),
            ],
            compiler_params=pltpu.CompilerParams(
                collective_id=0, has_side_effects=True, vmem_limit_bytes=24 << 20
            ),
        )(
            *(
                pltpu.with_memory_space_constraint(value, pltpu.HBM)
                for value in (
                    offsets,
                    phonon.T,
                    right_side,
                    rate,
                    fields,
                    speed.reshape(1, width),
                    regions,
                    contacts,
                )
            )
        )
        return pl.pallas_call(
            finish,
            out_shape=(
                jax.ShapeDtypeStruct(right_side.shape, f32),
                jax.ShapeDtypeStruct((SWEEPS, coefs), f32),
            ),
            in_specs=[vmem, vmem],
            out_specs=(hbm, hbm),
            scratch_shapes=[
                pltpu.VMEM((SWEEPS, coefs), f32),
                pltpu.SemaphoreType.DMA((coefs + 1,)),
            ],
            compiler_params=pltpu.CompilerParams(vmem_limit_bytes=8 << 20),
        )(state, sums)

    in_specs = (
        P(None, "space", None, "energy"),
        P("space", None, "energy"),
        P(None, "space", None),
        P("energy"),
        P("space", None),
        P("space", None),
        P(),
        P(),
    )
    out_specs = (P(None, "space", None, "energy"), P())
    return jax.shard_map(local, mesh=mesh, in_specs=in_specs, out_specs=out_specs, check_vma=False)
```
